512 devices in a mesh: band: 128 (over z_lo, y, x, core), head: 4 (over z_hi).
Axes of the slice: x: 4, y: 4, z: 16 (z_hi: 4, z_lo: 4; z = z_hi * 4 + z_lo), core: 2. Of those that a mesh axis runs over, the one named last changes fastest.
Arguments:
- queries: bfloat16 [256, 131072], P('head', 'band'), may hold values from -76 to 76
- keys: bfloat16 [256, 131072], P('head', 'band'), may hold values from -6 to 6
- values: bfloat16 [256, 131072], P('head', 'band'), may hold values from -6 to 6
- grad_out: bfloat16 [256, 131072], P('head', 'band'), may hold values from -6 to 6
- w_out: bfloat16 [256, 256], P('head'), may hold values from -0.375 to 0.375
- key_lists: int32 [1024, 8], P('band'), may hold values from 0 to 1023, as said below
- key_counts: int32 [1024], P('band'), may hold values from 2 to 8, as said below
Outputs:
- grad_queries: bfloat16 [256, 131072], P('head', 'band')
- grad_keys: bfloat16 [256, 131072], P('head', 'band')
- grad_values: bfloat16 [256, 131072], P('head', 'band')
- grad_w_out: float32 [256, 256], P('head')
The draws below stay inside these ranges and needn't reach their ends.
Inputs may be any that keep to these rules, and one draw needn't show every extreme that they name: `key_lists`: row b holds 8 different blocks; the first is b itself and every entry lies within 8 blocks of b. `key_counts`: the number of leading entries of the row of key_lists that are used.
All inputs are finite; a program needn't handle non-finite values.
Results may differ from the reference program's by a relative error of at most 0.0058.
Values may be sent and summed in bfloat16 or wider, within the bound.
A program may use at most 64 MiB of HBM per device.

```python
import jax
import jax.numpy as jnp
from jax import lax

D = 256
HEADS = 8
HEAD_DIM = 32
BLOCK = 128
REACH = 4
MAX_KEYS = 8
MIN_KEYS = 2
TOKENS = 131072
KEY_BLOCKS = 1024


def shared_fields(key):
    key_seed = jax.random.fold_in(key, 101)
    query_seed = jax.random.fold_in(key, 102)
    key_field = jnp.clip(jax.random.normal(key_seed, (TOKENS, D), jnp.float32), -6.0, 6.0)
    query_field = jnp.clip(jax.random.normal(query_seed, (TOKENS, D), jnp.float32), -6.0, 6.0)
    return (query_field, key_field)


def draw_queries(key, part):
    query_field, key_field = shared_fields(key)
    return query_field.T.astype(jnp.bfloat16)


def draw_keys(key, part):
    query_field, key_field = shared_fields(key)
    return key_field.T.astype(jnp.bfloat16)


def draw_key_lists(key, part):
    block_index = jnp.arange(KEY_BLOCKS, dtype=jnp.int32)
    window_low = jnp.clip(block_index - REACH, 0, KEY_BLOCKS - 1 - 2 * REACH)
    rank_seed = jax.random.fold_in(key, 201)
    scores = jax.random.randint(rank_seed, (KEY_BLOCKS, 2 * REACH), 0, 2 ** 20) * (2 * REACH) + jnp.arange(2 * REACH, dtype=jnp.int32)
    ranking = jnp.argsort(scores, axis=1).astype(jnp.int32)
    chosen = ranking[:, :MAX_KEYS - 1]
    offset = block_index - window_low
    others = window_low[:, None] + chosen + (chosen >= offset[:, None]).astype(jnp.int32)
    return jnp.concatenate([block_index[:, None], others], axis=1).astype(jnp.int32)


def draw_key_counts(key, part):
    block_index = jnp.arange(KEY_BLOCKS, dtype=jnp.int32)
    distance = jnp.minimum(block_index, KEY_BLOCKS - 1 - block_index)
    baseline = MAX_KEYS - (MAX_KEYS - MIN_KEYS) * 2 * distance // KEY_BLOCKS
    jitter = jax.random.randint(jax.random.fold_in(key, 301), (KEY_BLOCKS,), 0, 2) * (distance > 0).astype(jnp.int32)
    return jnp.clip(baseline - jitter, MIN_KEYS, MAX_KEYS).astype(jnp.int32)


def levels(rng, shape, split, smallest, largest):
    def one(axis_at, blocks):
        draws = jax.random.uniform(jax.random.fold_in(jax.random.fold_in(rng, 6), axis_at), (blocks,), jnp.float32, smallest / len(split), largest / len(split))
        return jnp.repeat(jnp.exp(draws), shape[axis_at] // blocks).reshape((-1,) + (1,) * (len(shape) - axis_at - 1))

    factor_of = one(*split[0])
    for cut in split[1:]:
        factor_of = factor_of * one(*cut)
    return factor_of


def centred(own_key, dims, scale, reach, shards=(), held_as=jnp.bfloat16):
    level = levels(own_key, dims, shards, -0.22, 0.18) if shards else 1.0
    values = jax.random.normal(own_key, dims, jnp.float32) * scale * level
    return jnp.minimum(jnp.maximum(values, -reach), reach).astype(held_as)


def setup_inputs(seed: int = 0) -> dict:
    streams_of = jax.random.split(jax.random.key(seed), 8)
    return {
        "queries": draw_queries(jax.random.fold_in(streams_of[7], 71), 0),
        "keys": draw_keys(jax.random.fold_in(streams_of[7], 71), 0),
        "values": centred(streams_of[2], (D, TOKENS), 1.0, 6.0, ((0, 4), (1, 128))),
        "grad_out": centred(streams_of[3], (D, TOKENS), 1.0, 6.0, ((0, 4), (1, 128))),
        "w_out": centred(streams_of[4], (D, D), D ** -0.5, 0.375, ((0, 4),)),
        "key_lists": draw_key_lists(jax.random.fold_in(streams_of[7], 71), 0),
        "key_counts": draw_key_counts(jax.random.fold_in(streams_of[7], 71), 0),
    }


def block_terms(query, grad, picked_k, picked_v, bias, live):
    scale = HEAD_DIM ** -0.5
    scores = jnp.einsum("qhd,khd->hqk", query, picked_k) * scale + bias
    scores = jnp.where(live, scores, -jnp.inf)
    peak = jnp.max(scores, axis=-1)
    log_total = peak + jnp.log(jnp.sum(jnp.exp(scores - peak[..., None]), axis=-1))
    probs = jnp.exp(scores - log_total[..., None])
    probs_low = lax.optimization_barrier(probs.astype(jnp.bfloat16)).astype(jnp.float32)
    dprobs = jnp.einsum("qhd,khd->hqk", grad, picked_v)
    spread = jnp.sum(probs * dprobs, axis=-1)
    dscores = (probs * (dprobs - spread[..., None]) * scale).astype(jnp.bfloat16)
    dscores = lax.optimization_barrier(dscores).astype(jnp.float32)
    dquery = jnp.einsum("hqk,khd->qhd", dscores, picked_k)
    dkey = jnp.einsum("hqk,qhd->khd", dscores, query)
    dvalue = jnp.einsum("hqk,qhd->khd", probs_low, grad)
    attended = jnp.einsum("hqk,khd->qhd", probs_low, picked_v)
    return dquery, dkey, dvalue, attended


def reference(queries, keys, values, grad_out, w_out, key_lists, key_counts):
    tokens = queries.shape[1]
    blocks = tokens // BLOCK
    grad_att = jnp.dot(w_out, grad_out, preferred_element_type=jnp.float32).astype(jnp.bfloat16).T
    positions = jnp.arange(tokens, dtype=jnp.int32).astype(jnp.float32)
    logw = jnp.log(jnp.sin(jnp.pi * (positions + 0.5) / tokens)).reshape(blocks, BLOCK)
    shape4 = (blocks, BLOCK, HEADS, HEAD_DIM)
    query_all = queries.T.reshape(shape4)
    key_all = keys.T.reshape(shape4)
    value_all = values.T.reshape(shape4)
    grad_all = grad_att.reshape(shape4)
    slot_ids = jnp.arange(MAX_KEYS, dtype=jnp.int32)
    span = MAX_KEYS * BLOCK

    def step(carry, block_id):
        acc_k, acc_v = carry
        slots = key_lists[block_id].astype(jnp.int32)
        live = jnp.repeat(slot_ids < key_counts[block_id], BLOCK)
        picked_k = key_all[slots].astype(jnp.float32).reshape(span, HEADS, HEAD_DIM)
        picked_v = value_all[slots].astype(jnp.float32).reshape(span, HEADS, HEAD_DIM)
        bias = logw[slots].reshape(span)
        query = query_all[block_id].astype(jnp.float32)
        grad = grad_all[block_id].astype(jnp.float32)
        dquery, dkey, dvalue, attended = block_terms(query, grad, picked_k, picked_v, bias, live)
        acc_k = acc_k.at[slots].add(dkey.reshape(MAX_KEYS, BLOCK, D))
        acc_v = acc_v.at[slots].add(dvalue.reshape(MAX_KEYS, BLOCK, D))
        return (acc_k, acc_v), (dquery.reshape(BLOCK, D).astype(jnp.bfloat16), attended.reshape(BLOCK, D).astype(jnp.bfloat16))

    zeros = jnp.zeros((blocks, BLOCK, D), jnp.float32)
    (acc_k, acc_v), (dq_blocks, att_blocks) = lax.scan(step, (zeros, zeros), jnp.arange(blocks, dtype=jnp.int32))
    grad_queries = dq_blocks.reshape(tokens, D).T
    grad_keys = acc_k.reshape(tokens, D).astype(jnp.bfloat16).T
    grad_values = acc_v.reshape(tokens, D).astype(jnp.bfloat16).T
    attended = att_blocks.reshape(tokens, D)
    grad_w_out = jnp.dot(attended.T, grad_out.T, preferred_element_type=jnp.float32)
    return (grad_queries, grad_keys, grad_values, grad_w_out)
```

```python
import math
import jax
import jax.numpy as jnp
from jax import lax
from jax.experimental import pallas as pl
from jax.experimental.pallas import tpu as pltpu
from jax.sharding import PartitionSpec as P

MESH = pl.DeviceIdType.MESH

def coords():
    me = lax.axis_index("band")
    core = lax.rem(me, 2); x = lax.rem(me // 2, 4); y = lax.rem(me // 8, 4); z = me // 32
    return core, x, y, z

def band_of(core, x, y, z):
    return ((z * 4 + y) * 4 + x) * 2 + core

def ar_kernel(w_ref, o_ref, part, r1, red, r2, tot, gat, s1, q1, s2, q2, s3, q3):
    core, x, y, z = coords()
    a = y * 4 + x
    plane = [(d, band_of(core, lax.rem(x + d % 4, 4), lax.rem(y + d // 4, 4), z),
              lax.rem(y + d // 4, 4) * 4 + lax.rem(x + d % 4, 4)) for d in range(1, 16)]
    line = [(d, band_of(lax.rem(core + d % 2, 2), x, y, lax.rem(z + d // 2, 4))) for d in range(1, 8)]
    barrier = pltpu.get_barrier_semaphore()
    for _, b, _ in plane:
        pl.semaphore_signal(barrier, inc=1, device_id={"band": b}, device_id_type=MESH)
    for _, b in line:
        pl.semaphore_signal(barrier, inc=1, device_id={"band": b}, device_id_type=MESH)
    w = w_ref[...]
    for t in range(16):
        part[t] = w[(t // 2) * 8:(t // 2) * 8 + 8, (t % 2) * 128:(t % 2) * 128 + 128]
    pl.semaphore_wait(barrier, 22)
    c1 = []
    for d, b, pa in plane:
        c = pltpu.make_async_remote_copy(src_ref=part.at[pa], dst_ref=r1.at[d], send_sem=s1.at[d], recv_sem=q1.at[d],
                                         device_id={"band": b}, device_id_type=MESH)
        c.start(); c1.append(c)
    for c in c1:
        c.wait_recv()
    acc = part[a]
    for d in range(1, 16):
        acc = acc + r1[d]
    red[...] = acc
    c2 = []
    for d, b in line:
        c = pltpu.make_async_remote_copy(src_ref=red, dst_ref=r2.at[d], send_sem=s2.at[d], recv_sem=q2.at[d],
                                         device_id={"band": b}, device_id_type=MESH)
        c.start(); c2.append(c)
    for c in c2:
        c.wait_recv()
    for d in range(1, 8):
        acc = acc + r2[d]
    tot[...] = acc
    gat[a] = acc
    c3 = []
    for d, b, pa in plane:
        c = pltpu.make_async_remote_copy(src_ref=tot, dst_ref=gat.at[a], send_sem=s3.at[d], recv_sem=q3.at[d],
                                         device_id={"band": b}, device_id_type=MESH)
        c.start(); c3.append(c)
    for c in c3:
        c.wait_recv()
    for t in range(16):
        o_ref[(t // 2) * 8:(t // 2) * 8 + 8, (t % 2) * 128:(t % 2) * 128 + 128] = gat[t]
    for c in c1 + c2 + c3:
        c.wait_send()

def ar(w):
    D = pltpu.SemaphoreType.DMA
    return pl.pallas_call(
        ar_kernel, out_shape=jax.ShapeDtypeStruct((64, 256), jnp.float32),
        in_specs=[pl.BlockSpec(memory_space=pltpu.VMEM)], out_specs=pl.BlockSpec(memory_space=pltpu.VMEM),
        scratch_shapes=[pltpu.VMEM((16, 8, 128), jnp.float32), pltpu.VMEM((16, 8, 128), jnp.float32), pltpu.VMEM((8, 128), jnp.float32),
                        pltpu.VMEM((8, 8, 128), jnp.float32), pltpu.VMEM((8, 128), jnp.float32), pltpu.VMEM((16, 8, 128), jnp.float32),
                        D((16,)), D((16,)), D((8,)), D((8,)), D((16,)), D((16,))],
        compiler_params=pltpu.CompilerParams(collective_id=0, has_side_effects=True),
        name="band_sum")(w)

SCALE = 32 ** -0.5
C = SCALE * math.log2(math.e)
F32, BF16 = jnp.float32, jnp.bfloat16

def dot(a, b):
    return jnp.dot(a, b, preferred_element_type=F32)

def dot_nt(a, b):
    return lax.dot_general(a, b, (((1,), (1,)), ((), ())), preferred_element_type=F32)

def fold(x):
    return x.reshape(16, 8, 256)

def head_diag(m):
    return jnp.concatenate([m[0:32, 0:128], m[32:64, 128:256]], axis=0)

def block_diag(m):
    z = jnp.zeros((32, 128), m.dtype)
    top = jnp.concatenate([m[0:32], z], axis=1)
    low = jnp.concatenate([z, m[32:64]], axis=1)
    return jnp.concatenate([top, low], axis=0)

def prep_block(e, k, v, bias_row, kv_fm, k_tm, v_tm):
    kv_fm[e, 0:64] = k
    kv_fm[e, 64:128] = v
    hi = bias_row.astype(BF16).astype(F32)
    mid = (bias_row - hi).astype(BF16).astype(F32)
    lo = (bias_row - hi) - mid
    row = lax.broadcasted_iota(jnp.int32, (64, 128), 0)
    aug = jnp.where(row == 0, hi, jnp.where(row == 1, mid, jnp.where(row == 2, lo, 0.0))).astype(BF16)
    k_tm[e] = jnp.concatenate([k, aug], axis=0).T
    v_tm[e] = jnp.concatenate([v, jnp.zeros((64, 128), BF16)], axis=0).T

def forward_block(b, q, eidx, kv_fm, k_tm, s_ref, p_ref, ps, inv_ref):
    qd = block_diag(q)
    qa = jnp.concatenate([qd, jnp.ones((64, 256), BF16)], axis=0)
    es = [eidx[b * 8 + j] for j in range(8)]
    top = None
    for j in range(8):
        s = dot(k_tm[es[j]], qa)
        s_ref[j] = s
        m8 = jnp.max(s.reshape(16, 8, 256), axis=0)
        top = m8 if top is None else jnp.maximum(top, m8)
    top = jnp.max(top, axis=0, keepdims=True) * C
    total = None
    for j in range(8):
        p = jnp.exp2(s_ref[j] * C - top)
        p_ref[b * 8 + j] = p
        l8 = jnp.sum(p.reshape(16, 8, 256), axis=0)
        total = l8 if total is None else total + l8
    inv = 1.0 / jnp.sum(total, axis=0, keepdims=True)
    inv_ref[b] = inv
    for j in range(8):
        ps[b * 8 + j, :, 256:512] = (p_ref[b * 8 + j] * inv).astype(BF16)
    v_all = jnp.concatenate([kv_fm[es[j], 64:128] for j in range(8)], axis=1)
    p_all = ps[pl.ds(b * 8, 8), :, 256:512].reshape(1024, 256)
    return head_diag(dot(v_all, p_all)).astype(BF16)

def backward_block(b, q, g, eidx, inv_idx, kv_fm, v_tm, d_ref, p_ref, ps, inv_ref, acc):
    gd = block_diag(g)
    ga = jnp.concatenate([gd, jnp.zeros((64, 256), BF16)], axis=0)
    es = [eidx[b * 8 + j] for j in range(8)]
    tot = None
    for j in range(8):
        d = dot(v_tm[es[j]], ga)
        d_ref[j] = d
        t8 = jnp.sum((p_ref[b * 8 + j] * d).reshape(16, 8, 256), axis=0)
        tot = t8 if tot is None else tot + t8
    inv = inv_ref[b]
    spread = jnp.sum(tot, axis=0, keepdims=True) * inv
    isc = inv * SCALE
    for j in range(8):
        ps[b * 8 + j, :, 0:256] = ((p_ref[b * 8 + j] * isc) * (d_ref[j] - spread)).astype(BF16)
    k_all = jnp.concatenate([kv_fm[es[j], 0:64] for j in range(8)], axis=1)
    d_all = ps[pl.ds(b * 8, 8), :, 0:256].reshape(1024, 256)
    dq = head_diag(dot(k_all, d_all)).astype(BF16)
    z = jnp.zeros((64, 256), BF16)
    w = jnp.concatenate([jnp.concatenate([block_diag(q), z], axis=1), jnp.concatenate([z, gd], axis=1)], axis=0)
    for i in range(17):
        acc[b + i] += dot_nt(ps[inv_idx[b * 17 + i]], w)
    return dq

def attn_kernel(eidx, inv_idx, bias, q_ref, kv_ref, grad_ref, w_out, dq_ref, acc, pw_ref,
                kv_fm, k_tm, v_tm, s_ref, p_ref, ps, inv_ref, att_ref):
    for e in range(24):
        prep_block(e, kv_ref[e // 8, 0, :, (e % 8) * 128:(e % 8 + 1) * 128], kv_ref[e // 8, 1, :, (e % 8) * 128:(e % 8 + 1) * 128],
                   bias[e:e + 1], kv_fm, k_tm, v_tm)
    zero = jnp.zeros((64, 128), BF16)
    prep_block(24, zero, zero, jnp.full((1, 128), -1e30, F32), kv_fm, k_tm, v_tm)
    ps[64] = jnp.zeros((128, 512), BF16)
    acc[...] = jnp.zeros_like(acc)

    def fwd(b, _):
        cols = pl.ds(pl.multiple_of(b * 128, 128), 128)
        att_ref[:, cols] = forward_block(b, q_ref[:, cols], eidx, kv_fm, k_tm, s_ref, p_ref, ps, inv_ref)
        return 0
    lax.fori_loop(0, 8, fwd, 0)

    def bwd(b, _):
        cols = pl.ds(pl.multiple_of(b * 128, 128), 128)
        g = dot(w_out[...], grad_ref[:, cols]).astype(BF16)
        dq_ref[:, cols] = backward_block(b, q_ref[:, cols], g, eidx, inv_idx, kv_fm, v_tm, s_ref, p_ref, ps, inv_ref, acc)
        return 0
    lax.fori_loop(0, 8, bwd, 0)
    pw_ref[...] = dot_nt(att_ref[...], grad_ref[...])

def attn(eidx, inv_idx, bias, q, kv, grad, w_out):
    V = pltpu.VMEM
    vs = pl.BlockSpec(memory_space=V)
    ss = pl.BlockSpec(memory_space=pltpu.SMEM)
    return pl.pallas_call(
        attn_kernel,
        out_shape=(jax.ShapeDtypeStruct((64, 1024), BF16), jax.ShapeDtypeStruct((24, 128, 128), F32), jax.ShapeDtypeStruct((64, 256), F32)),
        in_specs=[ss, ss, vs, vs, vs, vs, vs], out_specs=(vs, vs, vs),
        scratch_shapes=[V((25, 128, 128), BF16), V((25, 128, 128), BF16), V((25, 128, 128), BF16), V((8, 128, 256), F32),
                        V((64, 128, 256), F32), V((65, 128, 512), BF16), V((8, 1, 256), F32), V((64, 1024), BF16)],
        compiler_params=pltpu.CompilerParams(vmem_limit_bytes=60 * 2**20),
        name="attention_grads")(eidx, inv_idx, bias, q, kv, grad, w_out)


def shifted(value, steps):
    count = lax.axis_size("band")
    first, last = max(0, -steps), min(count, count - steps)
    return lax.ppermute(value, "band", [(i, i + steps) for i in range(first, last)])


def tables(key_lists, key_counts):
    first = lax.axis_index("band") * 8 - 8
    used = jnp.arange(8, dtype=jnp.int32)[None, :] < key_counts[:, None]
    local = key_lists - first
    eidx = jnp.where(used, local, 24)
    rows = jnp.arange(8, dtype=jnp.int32)[:, None]
    offset = jnp.where(used, local - rows, -1)
    hit = offset[:, None, :] == jnp.arange(17, dtype=jnp.int32)[None, :, None]
    tile = (rows * 8 + jnp.arange(8, dtype=jnp.int32)[None, :])[:, None, :]
    inv_idx = jnp.min(jnp.where(hit, tile, 64), axis=2)
    positions = first * 128 + jnp.arange(3072, dtype=jnp.int32)
    total = 1024 * lax.axis_size("band")
    positions = jnp.clip(positions, 0, total - 1).astype(jnp.float32)
    bias = jnp.log(jnp.sin(jnp.pi * (positions + 0.5) / total)).reshape(24, 128) * (32 ** 0.5)
    return eidx.reshape(-1), inv_idx.reshape(-1), bias


def shards(queries, keys, values, grad_out, w_out, key_lists, key_counts):
    full_grad = lax.all_gather(grad_out, "head", axis=0, tiled=True)
    pair = jnp.stack([keys, values])
    kv = jnp.stack([shifted(pair, 1), pair, shifted(pair, -1)])
    eidx, inv_idx, bias = tables(key_lists, key_counts)
    grad_queries, acc, partial_w = attn(eidx, inv_idx, bias, queries, kv, full_grad, w_out)
    grad_w_out = ar(partial_w)
    from_above = shifted(acc[:8].astype(BF16), -1).astype(F32)
    from_below = shifted(acc[16:].astype(BF16), 1).astype(F32)
    own = (acc[8:16] + from_above + from_below).astype(BF16)
    both = own.transpose(2, 0, 1).reshape(128, 1024)
    return grad_queries, both[:64], both[64:], grad_w_out


def solution(mesh):
    split = P("head", "band")
    in_specs = (split, split, split, split, P("head", None), P("band", None), P("band"))
    out_specs = (split, split, split, P("head", None))
    return jax.shard_map(shards, mesh=mesh, in_specs=in_specs, out_specs=out_specs, check_vma=False)
```

```python
import math
import jax
import jax.numpy as jnp
from jax import lax
from jax.experimental import pallas as pl
from jax.experimental.pallas import tpu as pltpu
from jax.sharding import PartitionSpec as P

MESH = pl.DeviceIdType.MESH
F32, BF16 = jnp.float32, jnp.bfloat16
SCALE = 32 ** -0.5
EXP2_SCALE = SCALE * math.log2(math.e)
PI_HIGH = 3.1415927410125732
PI_LOW = -8.742277657347586e-08


def dot(a, b):
    return jnp.dot(a, b, preferred_element_type=F32)


def dot_nt(a, b):
    return lax.dot_general(a, b, (((1,), (1,)), ((), ())), preferred_element_type=F32)


def head_diag(m):
    return jnp.concatenate([m[0:32, 0:128], m[32:64, 128:256]], axis=0)


def block_diag(m):
    z = jnp.zeros((32, 128), m.dtype)
    return jnp.concatenate(
        [jnp.concatenate([m[0:32], z], axis=1), jnp.concatenate([z, m[32:64]], axis=1)], axis=0
    )


def sin_to_pi(x):
    y = jnp.where(x > 0.5 * math.pi, (PI_HIGH - x) + PI_LOW, x)
    z = y * y
    r = jnp.full_like(y, 1.0 / math.factorial(13))
    for n in (11, 9, 7, 5, 3):
        r = r * z + (-1.0) ** ((n - 1) // 2) / math.factorial(n)
    return y + y * (z * r)


def prep_block(e, k, v, bias_row, kv_fm, k_tm, v_tm):
    kv_fm[e, 0:64] = k
    kv_fm[e, 64:128] = v
    high = bias_row.astype(BF16).astype(F32)
    mid = (bias_row - high).astype(BF16).astype(F32)
    low = (bias_row - high) - mid
    row = lax.broadcasted_iota(jnp.int32, (64, 128), 0)
    aug = jnp.where(row == 0, high, jnp.where(row == 1, mid, jnp.where(row == 2, low, 0.0)))
    k_tm[e] = jnp.concatenate([k, aug.astype(BF16)], axis=0).T
    v_tm[e] = jnp.concatenate([v, jnp.zeros((64, 128), BF16)], axis=0).T


def forward_block(b, q, eidx, kv_fm, k_tm, s_ref, p_ref, ps, inv_ref):
    qa = jnp.concatenate([block_diag(q), jnp.ones((64, 256), BF16)], axis=0)
    es = [eidx[b * 8 + j] for j in range(8)]
    top = None
    for j in range(8):
        s = dot(k_tm[es[j]], qa)
        s_ref[j] = s
        m8 = jnp.max(s.reshape(16, 8, 256), axis=0)
        top = m8 if top is None else jnp.maximum(top, m8)
    top = jnp.max(top, axis=0, keepdims=True) * EXP2_SCALE
    total = None
    for j in range(8):
        p = jnp.exp2(s_ref[j] * EXP2_SCALE - top)
        p_ref[b * 8 + j] = p
        l8 = jnp.sum(p.reshape(16, 8, 256), axis=0)
        total = l8 if total is None else total + l8
    inv = 1.0 / jnp.sum(total, axis=0, keepdims=True)
    inv_ref[b] = inv
    for j in range(8):
        ps[b * 8 + j, :, 256:512] = (p_ref[b * 8 + j] * inv).astype(BF16)
    v_all = jnp.concatenate([kv_fm[es[j], 64:128] for j in range(8)], axis=1)
    p_all = ps[pl.ds(b * 8, 8), :, 256:512].reshape(1024, 256)
    return head_diag(dot(v_all, p_all)).astype(BF16)


def backward_block(b, q, g, eidx, inv_idx, kv_fm, v_tm, d_ref, p_ref, ps, inv_ref, acc):
    gd = block_diag(g)
    ga = jnp.concatenate([gd, jnp.zeros((64, 256), BF16)], axis=0)
    es = [eidx[b * 8 + j] for j in range(8)]
    tot = None
    for j in range(8):
        d = dot(v_tm[es[j]], ga)
        d_ref[j] = d
        t8 = jnp.sum((p_ref[b * 8 + j] * d).reshape(16, 8, 256), axis=0)
        tot = t8 if tot is None else tot + t8
    inv = inv_ref[b]
    spread = jnp.sum(tot, axis=0, keepdims=True) * inv
    isc = inv * SCALE
    for j in range(8):
        ds = (p_ref[b * 8 + j] * isc) * (d_ref[j] - spread)
        ps[b * 8 + j, :, 0:256] = ds.astype(BF16)
    k_all = jnp.concatenate([kv_fm[es[j], 0:64] for j in range(8)], axis=1)
    d_all = ps[pl.ds(b * 8, 8), :, 0:256].reshape(1024, 256)
    dq = head_diag(dot(k_all, d_all)).astype(BF16)
    z = jnp.zeros((64, 256), BF16)
    w = jnp.concatenate(
        [jnp.concatenate([block_diag(q), z], axis=1), jnp.concatenate([z, gd], axis=1)], axis=0
    )
    for i in range(17):
        acc[b + i] += dot_nt(ps[inv_idx[b * 17 + i]], w)
    return dq


def chunk(b):
    return pl.ds(pl.multiple_of(b * 128, 128), 128)


def kernel(lists, counts, q_hbm, k_hbm, v_hbm, g_hbm, w_hbm, dq_hbm, dk_hbm, dv_hbm, dw_hbm,
           eidx, inv_idx, bias, qv, kvb, gfull, wv, kv_fm, k_tm, v_tm, s_ref, p_ref, ps, inv_ref, att, acc,
           dqv, dkv, halo_out, halo_in, pw, rc, xs, rx, mine, ry, ysum, rz, zsum, half, dwv,
           load_sem, ag_send, ag_recv, fw_send, fw_recv, kv_send, kv_recv, ho_send, ho_recv,
           c_send, c_recv, x_send, x_recv, y_send, y_recv, z_send, z_recv, a_send, a_recv, e_send, e_recv, out_sem):
    me = lax.axis_index("band")
    hi = lax.axis_index("head")
    core, x, y, z = lax.rem(me, 2), lax.rem(me // 2, 4), lax.rem(me // 8, 4), me // 32
    up, down = lax.rem(hi + 1, 4), lax.rem(hi + 3, 4)
    right, left = lax.rem(me + 1, 128), lax.rem(me + 127, 128)
    other = me + 1 - 2 * core
    x_of = [lax.rem(x + d, 4) for d in range(4)]
    xs_ids = [me + 2 * (x_of[d] - x) for d in range(4)]
    ys_ids = [me + 8 * (lax.rem(y + d, 4) - y) for d in range(4)]
    zs_ids = [me + 32 * (lax.rem(z + d, 4) - z) for d in range(4)]

    def remote(src, dst, send, recv, **to):
        return pltpu.make_async_remote_copy(src_ref=src, dst_ref=dst, send_sem=send, recv_sem=recv,
                                            device_id=to, device_id_type=MESH)

    barrier = pltpu.get_barrier_semaphore()
    for h in (up, down):
        pl.semaphore_signal(barrier, inc=1, device_id={"head": h}, device_id_type=MESH)
    for b in [left, right, other] + xs_ids[1:] + ys_ids[1:] + zs_ids[1:]:
        pl.semaphore_signal(barrier, inc=1, device_id={"band": b}, device_id_type=MESH)
    rows = pl.ds(pl.multiple_of(hi * 64, 64), 64)
    rows_below = pl.ds(pl.multiple_of(down * 64, 64), 64)
    rows_above = pl.ds(pl.multiple_of(up * 64, 64), 64)
    loads = [pltpu.make_async_copy(src, dst, load_sem.at[i]) for i, (src, dst) in enumerate([
        (g_hbm, gfull.at[rows]), (k_hbm, kvb.at[1, 0]), (v_hbm, kvb.at[1, 1]), (q_hbm, qv), (w_hbm, wv)])]
    for c in loads:
        c.start()

    def ag(c, way):
        return remote(gfull.at[rows, chunk(c)], gfull.at[rows, chunk(c)], ag_send.at[2 * c + way],
                      ag_recv.at[2 * c + way], head=(up, down)[way])

    def ag_arrived(c, way):
        src = (rows_below, rows_above)[way]
        return remote(gfull.at[src, chunk(c)], gfull.at[src, chunk(c)], ag_send.at[2 * c + way],
                      ag_recv.at[2 * c + way], head=(up, down)[way])

    rows_far = pl.ds(pl.multiple_of(lax.rem(hi + 2, 4) * 64, 64), 64)

    def fw(c):
        way = c % 2
        src = (rows_below, rows_above)[way]
        return remote(gfull.at[src, chunk(c)], gfull.at[src, chunk(c)], fw_send.at[c], fw_recv.at[c],
                      head=(up, down)[way])

    def fw_arrived(c):
        return remote(gfull.at[rows_far, chunk(c)], gfull.at[rows_far, chunk(c)], fw_send.at[c], fw_recv.at[c],
                      head=up)

    for c in loads[:3]:
        c.wait()
    pl.semaphore_wait(barrier, 14)
    for c in range(8):
        for way in range(2):
            ag(c, way).start()
    halos = [remote(kvb.at[1], kvb.at[0], kv_send.at[0], kv_recv.at[0], band=right),
             remote(kvb.at[1], kvb.at[2], kv_send.at[1], kv_recv.at[1], band=left)]
    for c in halos:
        c.start()

    first = me * 8 - 8

    def table(b, _):
        count = counts[b]
        es = []
        for j in range(8):
            e = jnp.where(j < count, lists[b, j] - first, 24)
            eidx[b * 8 + j] = e
            es.append(e)
        for i in range(17):
            t = jnp.int32(64)
            for j in range(8):
                t = jnp.where(es[j] == b + i, b * 8 + j, t)
            inv_idx[b * 17 + i] = t
        return 0
    lax.fori_loop(0, 8, table, 0)
    shape = (24, 128)
    pos = (first + lax.broadcasted_iota(jnp.int32, shape, 0)) * 128 + lax.broadcasted_iota(jnp.int32, shape, 1)
    pos = jnp.clip(pos, 0, 131071).astype(F32)
    bias[...] = jnp.log(sin_to_pi(math.pi * (pos + 0.5) / 131072)) * (32 ** 0.5)

    def prep(side):
        def one(i, _):
            e = side * 8 + i
            prep_block(e, kvb[side, 0, :, chunk(i)], kvb[side, 1, :, chunk(i)], bias[pl.ds(e, 1), :],
                       kv_fm, k_tm, v_tm)
            return 0
        lax.fori_loop(0, 8, one, 0)

    zero = jnp.zeros((64, 128), BF16)
    prep_block(24, zero, zero, jnp.full((1, 128), -1e30, F32), kv_fm, k_tm, v_tm)
    ps[64] = jnp.zeros((128, 512), BF16)
    acc[...] = jnp.zeros_like(acc)
    prep(1)
    halos[0].wait_recv()
    prep(0)
    halos[1].wait_recv()
    prep(2)
    loads[3].wait()
    loads[4].wait()

    def forward_chunk(c):
        ag_arrived(c, c % 2).wait_recv()
        fw(c).start()

    def fwd(b, _):
        att[:, chunk(b)] = forward_block(b, qv[:, chunk(b)], eidx, kv_fm, k_tm, s_ref, p_ref, ps, inv_ref)
        for at, cs in FORWARD_AT.items():
            @pl.when(b == at)
            def _():
                for c in cs:
                    forward_chunk(c)
        return 0
    lax.fori_loop(0, 8, fwd, 0)

    keep, give = core, 1 - core
    core_copy = remote(pw.at[give], rc, c_send.at[0], c_recv.at[0], band=other)
    x_copies = [remote(xs.at[x_of[d]], rx.at[d], x_send.at[d], x_recv.at[d], band=xs_ids[d]) for d in range(1, 4)]
    y_copies = [remote(mine, ry.at[d], y_send.at[d], y_recv.at[d], band=ys_ids[d]) for d in range(1, 4)]
    z_copies = [remote(ysum, rz.at[d], z_send.at[d], z_recv.at[d], band=zs_ids[d]) for d in range(1, 4)]
    a_copies = [remote(zsum, half.at[x], a_send.at[d], a_recv.at[d], band=xs_ids[d]) for d in range(1, 4)]
    a_waits = [remote(zsum, half.at[x_of[d]], a_send.at[d], a_recv.at[d], band=xs_ids[d]) for d in range(1, 4)]
    e_copy = remote(half, dwv.at[core], e_send.at[0], e_recv.at[0], band=other)
    e_wait = remote(half, dwv.at[give], e_send.at[0], e_recv.at[0], band=other)

    def sum_core():
        total = dot_nt(att[...], gfull[...])
        pw[0] = total[:, 0:128]
        pw[1] = total[:, 128:256]
        core_copy.start()

    def sum_x():
        core_copy.wait_recv()
        xs[...] = (pw[keep] + rc[...]).reshape(4, 16, 128)
        for c in x_copies:
            c.start()

    def sum_y():
        for c in x_copies:
            c.wait_recv()
        mine[...] = xs[x] + rx[1] + rx[2] + rx[3]
        for c in y_copies:
            c.start()

    def sum_z():
        for c in y_copies:
            c.wait_recv()
        ysum[...] = mine[...] + ry[1] + ry[2] + ry[3]
        for c in z_copies:
            c.start()

    def gather_x():
        for c in z_copies:
            c.wait_recv()
        t = ysum[...] + rz[1] + rz[2] + rz[3]
        zsum[...] = t
        half[x] = t
        for c in a_copies:
            c.start()

    def gather_core():
        for c in a_waits:
            c.wait_recv()
        e_copy.start()
        dwv[core] = half[...]

    def rest_of_chunk(c):
        ag_arrived(c, 1 - c % 2).wait_recv()
        fw_arrived(c).wait_recv()

    halo_copies = [remote(halo_out.at[0], halo_in.at[0], ho_send.at[0], ho_recv.at[0], band=left),
                   remote(halo_out.at[1], halo_in.at[1], ho_send.at[1], ho_recv.at[1], band=right)]

    def bwd(b, _):
        for at, cs in WAIT_AT.items():
            @pl.when(b == at)
            def _():
                for kind, c in cs:
                    (forward_chunk if kind else rest_of_chunk)(c)
        for at, step in SUM_AT.items():
            @pl.when(b == at)
            def _():
                {"core": sum_core, "x": sum_x, "y": sum_y, "z": sum_z}[step]()
        g = dot(wv[...], gfull[:, chunk(b)]).astype(BF16)
        dqv[:, chunk(b)] = backward_block(b, qv[:, chunk(b)], g, eidx, inv_idx, kv_fm, v_tm, s_ref, p_ref, ps,
                                          inv_ref, acc)
        return 0
    lax.fori_loop(0, 8, bwd, 0)
    outs = [pltpu.make_async_copy(dqv, dq_hbm, out_sem.at[0])]
    outs[0].start()
    halo_out[0] = acc[0:8].astype(BF16)
    halo_copies[0].start()
    halo_out[1] = acc[16:24].astype(BF16)
    halo_copies[1].start()
    for step in ("core", "x", "y", "z"):
        if step not in SUM_AT.values():
            {"core": sum_core, "x": sum_x, "y": sum_y, "z": sum_z}[step]()
    gather_x()
    for c in halo_copies:
        c.wait_recv()

    def finish(i, _):
        t = acc[8 + i] + halo_in[0, i].astype(F32) + halo_in[1, i].astype(F32)
        dkv[:, chunk(i)] = t.T.astype(BF16)
        return 0
    lax.fori_loop(0, 8, finish, 0)
    outs.append(pltpu.make_async_copy(dkv.at[0:64], dk_hbm, out_sem.at[1]))
    outs.append(pltpu.make_async_copy(dkv.at[64:128], dv_hbm, out_sem.at[2]))
    outs[1].start()
    outs[2].start()
    gather_core()
    e_wait.wait_recv()
    for i in range(2):
        c = pltpu.make_async_copy(dwv.at[i], dw_hbm.at[i], out_sem.at[3 + i])
        c.start()
        outs.append(c)
    for c in range(8):
        for way in range(2):
            ag(c, way).wait_send()
        fw(c).wait_send()
    for c in halos + halo_copies + [core_copy] + x_copies + y_copies + z_copies + a_copies + [e_copy]:
        c.wait_send()
    for c in outs:
        c.wait()


FORWARD_AT = {0: (0, 1), 2: (2,), 4: (3,), 6: (4,), 7: (5,)}
WAIT_AT = {0: ((1, 6), (0, 0)), 1: ((1, 7), (0, 1)), 2: ((0, 2),), 3: ((0, 3),),
           4: ((0, 4), (0, 5), (0, 6), (0, 7))}
SUM_AT = {4: "core", 5: "x", 7: "y"}


def shards(queries, keys, values, grad_out, w_out, key_lists, key_counts):
    V, S, D = pltpu.VMEM, pltpu.SMEM, pltpu.SemaphoreType.DMA
    hbm = pl.BlockSpec(memory_space=pl.ANY)
    smem = pl.BlockSpec(memory_space=S)
    slab = jax.ShapeDtypeStruct((64, 1024), BF16)
    piece = V((16, 128), F32)
    pieces = V((4, 16, 128), F32)
    dq, dk, dv, dw = pl.pallas_call(
        kernel,
        out_shape=(slab, slab, slab, jax.ShapeDtypeStruct((2, 4, 16, 128), F32)),
        in_specs=[smem, smem] + [hbm] * 5,
        out_specs=[hbm] * 4,
        scratch_shapes=[
            S((64,), jnp.int32), S((136,), jnp.int32), V((24, 128), F32), V((64, 1024), BF16),
            V((3, 2, 64, 1024), BF16), V((256, 1024), BF16), V((64, 256), BF16),
            V((25, 128, 128), BF16), V((25, 128, 128), BF16), V((25, 128, 128), BF16),
            V((8, 128, 256), F32), V((64, 128, 256), F32), V((65, 128, 512), BF16), V((8, 1, 256), F32),
            V((64, 1024), BF16), V((24, 128, 128), F32), V((64, 1024), BF16), V((128, 1024), BF16),
            V((2, 8, 128, 128), BF16), V((2, 8, 128, 128), BF16),
            V((2, 64, 128), F32), V((64, 128), F32), pieces, pieces, piece, pieces, piece, pieces, piece, pieces,
            V((2, 4, 16, 128), F32),
            D((5,)), D((16,)), D((16,)), D((8,)), D((8,)), D((2,)), D((2,)), D((2,)), D((2,)),
            D((1,)), D((1,)), D((4,)), D((4,)), D((4,)), D((4,)), D((4,)), D((4,)), D((4,)), D((4,)),
            D((1,)), D((1,)), D((5,)),
        ],
        compiler_params=pltpu.CompilerParams(collective_id=0, has_side_effects=True, vmem_limit_bytes=60 * 2**20),
        name="attention_grads",
    )(key_lists, key_counts, queries, keys, values, grad_out, w_out)
    dw = jnp.concatenate([dw[0].reshape(64, 128), dw[1].reshape(64, 128)], axis=1)
    return dq, dk, dv, dw


def solution(mesh):
    split = P("head", "band")
    in_specs = (split, split, split, split, P("head", None), P("band", None), P("band"))
    out_specs = (split, split, split, P("head", None))
    return jax.shard_map(shards, mesh=mesh, in_specs=in_specs, out_specs=out_specs, check_vma=False)
```

```python
import math
import jax
import jax.numpy as jnp
from jax import lax
from jax.experimental import pallas as pl
from jax.experimental.pallas import tpu as pltpu
from jax.sharding import PartitionSpec as P

MESH = pl.DeviceIdType.MESH
F32, BF16 = jnp.float32, jnp.bfloat16
SCALE = 32 ** -0.5
EXP2_SCALE = SCALE * math.log2(math.e)
PI_HIGH = 3.1415927410125732
PI_LOW = -8.742277657347586e-08


def dot(a, b):
    return jnp.dot(a, b, preferred_element_type=F32)


def dot_nt(a, b):
    return lax.dot_general(a, b, (((1,), (1,)), ((), ())), preferred_element_type=F32)


def head_diag(m):
    return jnp.concatenate([m[0:32, 0:128], m[32:64, 128:256]], axis=0)


def block_diag(m):
    z = jnp.zeros((32, 128), m.dtype)
    return jnp.concatenate(
        [jnp.concatenate([m[0:32], z], axis=1), jnp.concatenate([z, m[32:64]], axis=1)], axis=0
    )


def sin_to_pi(x):
    y = jnp.where(x > 0.5 * math.pi, (PI_HIGH - x) + PI_LOW, x)
    z = y * y
    r = jnp.full_like(y, 1.0 / math.factorial(13))
    for n in (11, 9, 7, 5, 3):
        r = r * z + (-1.0) ** ((n - 1) // 2) / math.factorial(n)
    return y + y * (z * r)


def prep_keys(e, k, bias_row, kv_fm, k_tm):
    kv_fm[e, 0:64] = k
    high = bias_row.astype(BF16).astype(F32)
    mid = (bias_row - high).astype(BF16).astype(F32)
    low = (bias_row - high) - mid
    row = lax.broadcasted_iota(jnp.int32, (64, 128), 0)
    aug = jnp.where(row == 0, high, jnp.where(row == 1, mid, jnp.where(row == 2, low, 0.0)))
    k_tm[e] = jnp.concatenate([k, aug.astype(BF16)], axis=0).T


def prep_values(e, v, kv_fm, v_tm):
    kv_fm[e, 64:128] = v
    v_tm[e] = jnp.concatenate([v, jnp.zeros((64, 128), BF16)], axis=0).T


def forward_block(b, q, eidx, kv_fm, k_tm, s_ref, p_ref, ps, inv_ref):
    qa = jnp.concatenate([block_diag(q), jnp.ones((64, 256), BF16)], axis=0)
    es = [eidx[b * 8 + j] for j in range(8)]
    top = None
    for j in range(8):
        s = dot(k_tm[es[j]], qa)
        s_ref[j] = s
        m8 = jnp.max(s.reshape(16, 8, 256), axis=0)
        top = m8 if top is None else jnp.maximum(top, m8)
    top = jnp.max(top, axis=0, keepdims=True) * EXP2_SCALE
    total = None
    for j in range(8):
        p = jnp.exp2(s_ref[j] * EXP2_SCALE - top)
        p_ref[b * 8 + j] = p
        l8 = jnp.sum(p.reshape(16, 8, 256), axis=0)
        total = l8 if total is None else total + l8
    inv = 1.0 / jnp.sum(total, axis=0, keepdims=True)
    inv_ref[b] = inv
    for j in range(8):
        ps[b * 8 + j, :, 256:512] = (p_ref[b * 8 + j] * inv).astype(BF16)


def attended_block(b, eidx, kv_fm, ps):
    v_all = jnp.concatenate([kv_fm[eidx[b * 8 + j], 64:128] for j in range(8)], axis=1)
    p_all = ps[pl.ds(b * 8, 8), :, 256:512].reshape(1024, 256)
    return head_diag(dot(v_all, p_all)).astype(BF16)


def backward_block(b, q, g, eidx, inv_idx, kv_fm, v_tm, d_ref, p_ref, ps, inv_ref, acc, tmp, middle):
    gd = block_diag(g)
    ga = jnp.concatenate([gd, jnp.zeros((64, 256), BF16)], axis=0)
    es = [eidx[b * 8 + j] for j in range(8)]
    tot = None
    for j in range(8):
        d = dot(v_tm[es[j]], ga)
        d_ref[j] = d
        t8 = jnp.sum((p_ref[b * 8 + j] * d).reshape(16, 8, 256), axis=0)
        tot = t8 if tot is None else tot + t8
    inv = inv_ref[b]
    spread = jnp.sum(tot, axis=0, keepdims=True) * inv
    isc = inv * SCALE
    for j in range(8):
        ds = (p_ref[b * 8 + j] * isc) * (d_ref[j] - spread)
        ps[b * 8 + j, :, 0:256] = ds.astype(BF16)
    k_all = jnp.concatenate([kv_fm[es[j], 0:64] for j in range(8)], axis=1)
    d_all = ps[pl.ds(b * 8, 8), :, 0:256].reshape(1024, 256)
    dq = head_diag(dot(k_all, d_all)).astype(BF16)
    z = jnp.zeros((64, 256), BF16)
    w = jnp.concatenate(
        [jnp.concatenate([block_diag(q), z], axis=1), jnp.concatenate([z, gd], axis=1)], axis=0
    )
    middle()
    tmp[0:8] = dot(ps[pl.ds(b * 8, 8)].reshape(1024, 512), w.T).reshape(8, 128, 128)
    for i in range(17):
        acc[b + i] += tmp[inv_idx[b * 17 + i]]
    return dq


def chunk(b):
    return pl.ds(pl.multiple_of(b * 128, 128), 128)


def kernel(lists, counts, q_hbm, k_hbm, v_hbm, g_hbm, w_hbm, grads_hbm, dw_hbm,
           eidx, inv_idx, bias, qv, kvb, gfull, wv, kv_fm, k_tm, v_tm, s_ref, p_ref, ps, inv_ref, att, acc, tmp,
           dqv, dkv, halo_out, halo_in, pw, rc, xs, rx, mine, ry, ysum, rz, zsum, half, dwv,
           load_sem, ag_send, ag_recv, fw_send, fw_recv, kv_send, kv_recv, ho_send, ho_recv,
           c_send, c_recv, x_send, x_recv, y_send, y_recv, z_send, z_recv, a_send, a_recv, e_send, e_recv, out_sem, go):
    me = lax.axis_index("band")
    hi = lax.axis_index("head")
    core, x, y, z = lax.rem(me, 2), lax.rem(me // 2, 4), lax.rem(me // 8, 4), me // 32
    up, down = lax.rem(hi + 1, 4), lax.rem(hi + 3, 4)
    right, left = lax.rem(me + 1, 128), lax.rem(me + 127, 128)
    other = me + 1 - 2 * core
    x_of = [lax.rem(x + d, 4) for d in range(4)]
    xs_ids = [me + 2 * (x_of[d] - x) for d in range(4)]
    ys_ids = [me + 8 * (lax.rem(y + d, 4) - y) for d in range(4)]
    zs_ids = [me + 32 * (lax.rem(z + d, 4) - z) for d in range(4)]

    def remote(src, dst, send, recv, **to):
        return pltpu.make_async_remote_copy(src_ref=src, dst_ref=dst, send_sem=send, recv_sem=recv,
                                            device_id=to, device_id_type=MESH)

    barrier = pltpu.get_barrier_semaphore()
    for h in (up, down):
        pl.semaphore_signal(barrier, inc=1, device_id={"head": h}, device_id_type=MESH)
    for b in [left, right, other] + xs_ids[1:] + ys_ids[1:] + zs_ids[1:]:
        pl.semaphore_signal(barrier, inc=1, device_id={"band": b}, device_id_type=MESH)
    rows = pl.ds(pl.multiple_of(hi * 64, 64), 64)
    loads = [pltpu.make_async_copy(src, dst, load_sem.at[i]) for i, (src, dst) in enumerate([
        (k_hbm, kvb.at[1, 0]), (v_hbm, kvb.at[1, 1]), (q_hbm, qv), (w_hbm, wv), (g_hbm, gfull.at[rows])])]
    for c in loads:
        c.start()

    column_low, column_high = x + y == 0, x + y == 6

    def ag(c, way):
        return remote(g_hbm.at[:, chunk(c)], gfull.at[rows, chunk(c)], ag_send.at[2 * c + way],
                      ag_recv.at[2 * c + way], head=(up, down)[way])

    rows_far = pl.ds(pl.multiple_of(lax.rem(hi + 2, 4) * 64, 64), 64)

    def way_of(c):
        far_low, far_high = (0, 1)
        way = lax.rem(c, 2)
        way = jnp.where(jnp.logical_and(column_low, c == 7), far_low, way)
        return jnp.where(jnp.logical_and(column_high, c == 6), far_high, way)

    def rows_from(way):
        return pl.ds(pl.multiple_of(jnp.where(way == 0, down, up) * 64, 64), 64)

    def fw(c):
        way = way_of(c)
        src = rows_from(way)
        return remote(gfull.at[src, chunk(c)], gfull.at[src, chunk(c)], fw_send.at[c], fw_recv.at[c],
                      head=jnp.where(way == 0, up, down))

    def fw_arrived(c):
        return remote(gfull.at[rows_far, chunk(c)], gfull.at[rows_far, chunk(c)], fw_send.at[c], fw_recv.at[c],
                      head=up)

    first = me * 8 - 8

    def table(b, _):
        count = counts[b]
        es = []
        for j in range(8):
            e = jnp.where(j < count, lists[b, j] - first, 24)
            eidx[b * 8 + j] = e
            es.append(e)
        for i in range(17):
            t = jnp.int32(8)
            for j in range(8):
                t = jnp.where(es[j] == b + i, j, t)
            inv_idx[b * 17 + i] = t
        return 0
    lax.fori_loop(0, 8, table, 0)
    shape = (24, 128)
    pos = (first + lax.broadcasted_iota(jnp.int32, shape, 0)) * 128 + lax.broadcasted_iota(jnp.int32, shape, 1)
    pos = jnp.clip(pos, 0, 131071).astype(F32)
    bias[...] = jnp.log(sin_to_pi(math.pi * (pos + 0.5) / 131072)) * (32 ** 0.5)

    has_left, has_right = me > 0, me < 127

    def halo(side, i):
        return remote((k_hbm, v_hbm)[i], kvb.at[side, i], kv_send.at[side + i], kv_recv.at[side + i],
                      band=right if side == 0 else left)

    pl.semaphore_wait(barrier, 14)

    @pl.when(has_right)
    def _():
        for i in range(2):
            halo(0, i).start()

    @pl.when(has_left)
    def _():
        for i in range(2):
            halo(2, i).start()

    def start_gather(ways):
        for c in range(8):
            for way in ways:
                ag(c, way).start()

    column = jnp.logical_or(x + y == 0, x + y == 6)
    paired = jnp.logical_and(column, jnp.where(x == 0, z > 0, z < 3))
    crossing = jnp.logical_and(paired, core == jnp.where(x == 0, 0, 1))
    cross_low = jnp.logical_and(crossing, core == 0)
    cross_high = jnp.logical_and(crossing, core == 1)
    pl.when(jnp.logical_not(column))(lambda: start_gather((0, 1)))
    pl.when(column_low)(lambda: start_gather((0,)))
    pl.when(column_high)(lambda: start_gather((1,)))

    def keys_of(side):
        def one(i, _):
            e = side * 8 + i
            prep_keys(e, kvb[side, 0, :, chunk(i)], bias[pl.ds(e, 1), :], kv_fm, k_tm)
            return 0
        lax.fori_loop(0, 8, one, 0)

    def values_of(side):
        def one(i, _):
            prep_values(side * 8 + i, kvb[side, 1, :, chunk(i)], kv_fm, v_tm)
            return 0
        lax.fori_loop(0, 8, one, 0)

    zero = jnp.zeros((64, 128), BF16)
    prep_keys(24, zero, jnp.full((1, 128), -1e30, F32), kv_fm, k_tm)
    prep_values(24, zero, kv_fm, v_tm)
    tmp[8] = jnp.zeros((128, 128), F32)
    acc[...] = jnp.zeros_like(acc)
    for i in range(4):
        loads[i].wait()
    keys_of(1)
    values_of(1)

    pl.when(cross_low)(lambda: halo(2, 0).wait_send())
    pl.when(cross_high)(lambda: halo(0, 0).wait_send())

    @pl.when(crossing)
    def _():
        pl.semaphore_signal(go, inc=1, device_id={"band": other}, device_id_type=MESH)

    @pl.when(jnp.logical_and(paired, jnp.logical_not(crossing)))
    def _():
        pl.semaphore_wait(go, 1)
    pl.when(column_low)(lambda: start_gather((1,)))
    pl.when(column_high)(lambda: start_gather((0,)))

    def arrived(side, i, prep):
        halo(side, i).wait_recv()
        prep(side)
    pl.when(has_left)(lambda: arrived(0, 0, keys_of))
    pl.when(has_right)(lambda: arrived(2, 0, keys_of))

    def ag_arrived(c, way):
        src = rows_from(way)
        return remote(gfull.at[src, chunk(c)], gfull.at[src, chunk(c)], ag_send.at[2 * c + way],
                      ag_recv.at[2 * c + way], head=jnp.where(way == 0, up, down))

    def forward_chunk(c):
        ag_arrived(c, way_of(c)).wait_recv()
        fw(c).start()

    def fwd(b, _):
        forward_block(b, qv[:, chunk(b)], eidx, kv_fm, k_tm, s_ref, p_ref, ps, inv_ref)
        for at, cs in FORWARD_AT.items():
            @pl.when(jnp.logical_and(b == at, jnp.logical_not(column)))
            def _():
                for c in cs:
                    forward_chunk(c)
        return 0
    lax.fori_loop(0, 8, fwd, 0)
    pl.when(has_left)(lambda: arrived(0, 1, values_of))
    pl.when(has_right)(lambda: arrived(2, 1, values_of))

    def attend(b, _):
        att[:, chunk(b)] = attended_block(b, eidx, kv_fm, ps)
        return 0
    lax.fori_loop(0, 8, attend, 0)

    @pl.when(column)
    def _():
        for c in range(8):
            forward_chunk(c)

    @pl.when(jnp.logical_not(column))
    def _():
        for c in FORWARD_LAST:
            forward_chunk(c)

    keep, give = core, 1 - core
    core_copy = remote(pw.at[give], rc, c_send.at[0], c_recv.at[0], band=other)
    x_copies = [remote(xs.at[x_of[d]], rx.at[d], x_send.at[d], x_recv.at[d], band=xs_ids[d]) for d in range(1, 4)]
    y_copies = [remote(mine, ry.at[d], y_send.at[d], y_recv.at[d], band=ys_ids[d]) for d in range(1, 4)]
    z_copies = [remote(ysum, rz.at[d], z_send.at[d], z_recv.at[d], band=zs_ids[d]) for d in range(1, 4)]
    a_copies = [remote(zsum, half.at[x], a_send.at[d], a_recv.at[d], band=xs_ids[d]) for d in range(1, 4)]
    a_waits = [remote(zsum, half.at[x_of[d]], a_send.at[d], a_recv.at[d], band=xs_ids[d]) for d in range(1, 4)]
    e_copy = remote(half, dwv.at[core], e_send.at[0], e_recv.at[0], band=other)
    e_wait = remote(half, dwv.at[give], e_send.at[0], e_recv.at[0], band=other)

    def sum_core():
        total = dot_nt(att[...], gfull[...])
        pw[0] = total[:, 0:128]
        pw[1] = total[:, 128:256]
        core_copy.start()

    def sum_x():
        core_copy.wait_recv()
        xs[...] = (pw[keep] + rc[...]).reshape(4, 16, 128)
        for c in x_copies:
            c.start()

    def sum_y():
        for c in x_copies:
            c.wait_recv()
        mine[...] = xs[x] + rx[1] + rx[2] + rx[3]
        for c in y_copies:
            c.start()

    def sum_z():
        for c in y_copies:
            c.wait_recv()
        ysum[...] = mine[...] + ry[1] + ry[2] + ry[3]
        for c in z_copies:
            c.start()

    def gather_x():
        for c in z_copies:
            c.wait_recv()
        t = ysum[...] + rz[1] + rz[2] + rz[3]
        zsum[...] = t
        half[x] = t
        for c in a_copies:
            c.start()

    def gather_core():
        for c in a_waits:
            c.wait_recv()
        e_copy.start()
        dwv[core] = half[...]

    def rest_of_chunk(c):
        ag_arrived(c, 1 - way_of(c)).wait_recv()
        fw_arrived(c).wait_recv()

    start = jnp.where(column, START_LATE, START)

    def halo_back(side, i):
        return remote(halo_out.at[side, i], halo_in.at[side, i], ho_send.at[side * 8 + i], ho_recv.at[side * 8 + i],
                      band=(left, right)[side])

    steps = {"core": sum_core, "x": sum_x, "y": sum_y, "z": sum_z}

    def bwd(b, _):
        pl.when(b < start)(lambda: rest_of_chunk(b))

        @pl.when(b == start)
        def _():
            pl.loop(b, 8)(rest_of_chunk)

        def serve(mid):
            for at, step in SUM_AT.items():
                if at % 2 == mid:
                    pl.when(b == start + at // 2)(steps[step])
        serve(0)
        g = dot(wv[...], gfull[:, chunk(b)]).astype(BF16)
        dqv[:, chunk(b)] = backward_block(b, qv[:, chunk(b)], g, eidx, inv_idx, kv_fm, v_tm, s_ref, p_ref, ps,
                                          inv_ref, acc, tmp, lambda: serve(1))
        @pl.when(has_left)
        def _():
            halo_out[0, b] = acc[b].astype(BF16)
            halo_back(0, b).start()
        return 0
    loads[4].wait()
    lax.fori_loop(0, 8, bwd, 0)

    def send_upper(i, _):
        halo_out[1, i] = acc[16 + i].astype(BF16)
        halo_back(1, i).start()
        return 0

    @pl.when(has_right)
    def _():
        lax.fori_loop(0, 8, send_upper, 0)
    outs = [pltpu.make_async_copy(dqv, grads_hbm.at[0], out_sem.at[0])]
    outs[0].start()
    for step in ("core", "x", "y", "z"):
        if step not in SUM_AT.values():
            steps[step]()
    gather_x()

    @pl.when(jnp.logical_not(has_right))
    def _():
        halo_in[0] = jnp.zeros((8, 128, 128), BF16)

    @pl.when(jnp.logical_not(has_left))
    def _():
        halo_in[1] = jnp.zeros((8, 128, 128), BF16)

    def finish(i, _):
        pl.when(has_right)(lambda: halo_back(0, i).wait_recv())
        pl.when(has_left)(lambda: halo_back(1, i).wait_recv())
        t = acc[8 + i] + halo_in[0, i].astype(F32) + halo_in[1, i].astype(F32)
        dkv[:, chunk(i)] = t.T.astype(BF16)
        return 0
    lax.fori_loop(0, 8, finish, 0)
    outs.append(pltpu.make_async_copy(dkv.at[0:64], grads_hbm.at[1], out_sem.at[1]))
    outs.append(pltpu.make_async_copy(dkv.at[64:128], grads_hbm.at[2], out_sem.at[2]))
    outs[1].start()
    outs[2].start()
    gather_core()
    e_wait.wait_recv()
    for i in range(2):
        for r in range(4):
            c = pltpu.make_async_copy(dwv.at[i, r], dw_hbm.at[r * 16:r * 16 + 16, i * 128:i * 128 + 128], out_sem.at[3 + i * 4 + r])
            c.start()
            outs.append(c)
    for c in range(8):
        for way in range(2):
            ag(c, way).wait_send()
        fw(c).wait_send()

    @pl.when(has_left)
    def _():
        for c in range(8):
            halo_back(0, c).wait_send()

    pl.when(jnp.logical_and(has_left, jnp.logical_not(cross_low)))(lambda: halo(2, 0).wait_send())
    pl.when(has_left)(lambda: halo(2, 1).wait_send())

    @pl.when(has_right)
    def _():
        for c in range(8):
            halo_back(1, c).wait_send()

    pl.when(jnp.logical_and(has_right, jnp.logical_not(cross_high)))(lambda: halo(0, 0).wait_send())
    pl.when(has_right)(lambda: halo(0, 1).wait_send())

    for c in [core_copy] + x_copies + y_copies + z_copies + a_copies + [e_copy]:
        c.wait_send()
    for c in outs:
        c.wait()


FORWARD_AT = {3: (0,), 5: (1,), 7: (2, 3)}
FORWARD_LAST = (4, 5, 6, 7)
START, START_LATE = 3, 3
SUM_AT = {0: "core", 2: "x", 6: "y"}


def shards(queries, keys, values, grad_out, w_out, key_lists, key_counts):
    V, S, D = pltpu.VMEM, pltpu.SMEM, pltpu.SemaphoreType.DMA
    hbm = pl.BlockSpec(memory_space=pl.ANY)
    smem = pl.BlockSpec(memory_space=S)
    slab = jax.ShapeDtypeStruct((64, 1024), BF16)
    piece = V((16, 128), F32)
    pieces = V((4, 16, 128), F32)
    grads, dw = pl.pallas_call(
        kernel,
        out_shape=(jax.ShapeDtypeStruct((3, 64, 1024), BF16), jax.ShapeDtypeStruct((64, 256), F32)),
        in_specs=[smem, smem] + [hbm] * 5,
        out_specs=[hbm] * 2,
        scratch_shapes=[
            S((64,), jnp.int32), S((136,), jnp.int32), V((24, 128), F32), V((64, 1024), BF16),
            V((3, 2, 64, 1024), BF16), V((256, 1024), BF16), V((64, 256), BF16),
            V((25, 128, 128), BF16), V((25, 128, 128), BF16), V((25, 128, 128), BF16),
            V((8, 128, 256), F32), V((64, 128, 256), F32), V((64, 128, 512), BF16), V((8, 1, 256), F32),
            V((64, 1024), BF16), V((24, 128, 128), F32), V((9, 128, 128), F32), V((64, 1024), BF16), V((128, 1024), BF16),
            V((2, 8, 128, 128), BF16), V((2, 8, 128, 128), BF16),
            V((2, 64, 128), F32), V((64, 128), F32), pieces, pieces, piece, pieces, piece, pieces, piece, pieces,
            V((2, 4, 16, 128), F32),
            D((5,)), D((16,)), D((16,)), D((8,)), D((8,)), D((4,)), D((4,)), D((16,)), D((16,)),
            D((1,)), D((1,)), D((4,)), D((4,)), D((4,)), D((4,)), D((4,)), D((4,)), D((4,)), D((4,)),
            D((1,)), D((1,)), D((11,)), pltpu.SemaphoreType.REGULAR,
        ],
        compiler_params=pltpu.CompilerParams(collective_id=0, has_side_effects=True, vmem_limit_bytes=60 * 2**20),
        name="attention_grads",
    )(key_lists, key_counts, queries, keys, values, grad_out, w_out)
    return grads[0], grads[1], grads[2], dw


def solution(mesh):
    split = P("head", "band")
    in_specs = (split, split, split, split, P("head", None), P("band", None), P("band"))
    out_specs = (split, split, split, P("head", None))
    return jax.shard_map(shards, mesh=mesh, in_specs=in_specs, out_specs=out_specs, check_vma=False)
```

```python
import math
import jax
import jax.numpy as jnp
from jax import lax
from jax.experimental import pallas as pl
from jax.experimental.pallas import tpu as pltpu
from jax.sharding import PartitionSpec as P

MESH = pl.DeviceIdType.MESH
F32, BF16 = jnp.float32, jnp.bfloat16
SCALE = 32 ** -0.5
EXP2_SCALE = SCALE * math.log2(math.e)
PI_HIGH = 3.1415927410125732
PI_LOW = -8.742277657347586e-08


def dot(a, b):
    return jnp.dot(a, b, preferred_element_type=F32)


def dot_nt(a, b):
    return lax.dot_general(a, b, (((1,), (1,)), ((), ())), preferred_element_type=F32)


def head_diag(m):
    return jnp.concatenate([m[0:32, 0:128], m[32:64, 128:256]], axis=0)


def block_diag(m):
    z = jnp.zeros((32, 128), m.dtype)
    return jnp.concatenate(
        [jnp.concatenate([m[0:32], z], axis=1), jnp.concatenate([z, m[32:64]], axis=1)], axis=0
    )


def sin_to_pi(x):
    y = jnp.where(x > 0.5 * math.pi, (PI_HIGH - x) + PI_LOW, x)
    z = y * y
    r = jnp.full_like(y, 1.0 / math.factorial(13))
    for n in (11, 9, 7, 5, 3):
        r = r * z + (-1.0) ** ((n - 1) // 2) / math.factorial(n)
    return y + y * (z * r)


def prep_keys(e, k, bias_row, kv_fm, k_tm):
    kv_fm[e, 0:64] = k
    high = bias_row.astype(BF16).astype(F32)
    mid = (bias_row - high).astype(BF16).astype(F32)
    low = (bias_row - high) - mid
    row = lax.broadcasted_iota(jnp.int32, (64, 128), 0)
    aug = jnp.where(row == 0, high, jnp.where(row == 1, mid, jnp.where(row == 2, low, 0.0)))
    k_tm[e] = jnp.concatenate([k, aug.astype(BF16)], axis=0).T


def prep_values(e, v, kv_fm, v_tm):
    kv_fm[e, 64:128] = v
    v_tm[e] = jnp.concatenate([v, jnp.zeros((64, 128), BF16)], axis=0).T


def forward_block(b, q, eidx, kv_fm, k_tm, s_ref, p_ref, ps, inv_ref):
    qa = jnp.concatenate([block_diag(q), jnp.ones((64, 256), BF16)], axis=0)
    es = [eidx[b * 8 + j] for j in range(8)]
    top = None
    for j in range(8):
        s = dot(k_tm[es[j]], qa)
        s_ref[j] = s
        m8 = jnp.max(s.reshape(16, 8, 256), axis=0)
        top = m8 if top is None else jnp.maximum(top, m8)
    top = jnp.max(top, axis=0, keepdims=True) * EXP2_SCALE
    total = None
    for j in range(8):
        p = jnp.exp2(s_ref[j] * EXP2_SCALE - top)
        p_ref[b * 8 + j] = p
        l8 = jnp.sum(p.reshape(16, 8, 256), axis=0)
        total = l8 if total is None else total + l8
    inv = 1.0 / jnp.sum(total, axis=0, keepdims=True)
    inv_ref[b] = inv
    for j in range(8):
        ps[b * 8 + j, :, 256:512] = (p_ref[b * 8 + j] * inv).astype(BF16)


def attended_block(b, eidx, kv_fm, ps):
    v_all = jnp.concatenate([kv_fm[eidx[b * 8 + j], 64:128] for j in range(8)], axis=1)
    p_all = ps[pl.ds(b * 8, 8), :, 256:512].reshape(1024, 256)
    return head_diag(dot(v_all, p_all)).astype(BF16)


def backward_block(b, q, g, eidx, inv_idx, kv_fm, v_tm, d_ref, p_ref, ps, inv_ref, acc, tmp, middle):
    gd = block_diag(g)
    ga = jnp.concatenate([gd, jnp.zeros((64, 256), BF16)], axis=0)
    es = [eidx[b * 8 + j] for j in range(8)]
    tot = None
    for j in range(8):
        d = dot(v_tm[es[j]], ga)
        d_ref[j] = d
        t8 = jnp.sum((p_ref[b * 8 + j] * d).reshape(16, 8, 256), axis=0)
        tot = t8 if tot is None else tot + t8
    inv = inv_ref[b]
    spread = jnp.sum(tot, axis=0, keepdims=True) * inv
    isc = inv * SCALE
    for j in range(8):
        ds = (p_ref[b * 8 + j] * isc) * (d_ref[j] - spread)
        ps[b * 8 + j, :, 0:256] = ds.astype(BF16)
    k_all = jnp.concatenate([kv_fm[es[j], 0:64] for j in range(8)], axis=1)
    d_all = ps[pl.ds(b * 8, 8), :, 0:256].reshape(1024, 256)
    dq = head_diag(dot(k_all, d_all)).astype(BF16)
    z = jnp.zeros((64, 256), BF16)
    w = jnp.concatenate(
        [jnp.concatenate([block_diag(q), z], axis=1), jnp.concatenate([z, gd], axis=1)], axis=0
    )
    middle()
    tmp[0:8] = dot(ps[pl.ds(b * 8, 8)].reshape(1024, 512), w.T).reshape(8, 128, 128)
    for i in range(17):
        acc[b + i] += tmp[inv_idx[b * 17 + i]]
    return dq


def chunk(b):
    return pl.ds(pl.multiple_of(b * 128, 128), 128)


def kernel(lists_hbm, counts_hbm, q_hbm, k_hbm, v_hbm, g_hbm, w_hbm, grads_hbm, dw_hbm,
           lists, counts, eidx, inv_idx, bias, qv, kvb, gfull, wv, kv_fm, k_tm, v_tm, s_ref, p_ref, ps, inv_ref, att, acc, tmp,
           dqv, dkv, halo_out, halo_in, pw, rc, xs, rx, mine, ry, ysum, rz, zsum, half,
           load_sem, ag_send, ag_recv, fw_send, fw_recv, kv_send, kv_recv, ho_send, ho_recv,
           c_send, c_recv, x_send, x_recv, y_send, y_recv, z_send, z_recv, a_send, a_recv, e_send, e_recv, out_sem):
    me = lax.axis_index("band")
    hi = lax.axis_index("head")
    core, x, y, z = lax.rem(me, 2), lax.rem(me // 2, 4), lax.rem(me // 8, 4), me // 32
    up, down = lax.rem(hi + 1, 4), lax.rem(hi + 3, 4)
    right, left = lax.rem(me + 1, 128), lax.rem(me + 127, 128)
    other = me + 1 - 2 * core
    x_of = [lax.rem(x + d, 4) for d in range(4)]
    xs_ids = [me + 2 * (x_of[d] - x) for d in range(4)]
    ys_ids = [me + 8 * (lax.rem(y + d, 4) - y) for d in range(4)]
    zs_ids = [me + 32 * (lax.rem(z + d, 4) - z) for d in range(4)]

    def remote(src, dst, send, recv, **to):
        return pltpu.make_async_remote_copy(src_ref=src, dst_ref=dst, send_sem=send, recv_sem=recv,
                                            device_id=to, device_id_type=MESH)

    barrier = pltpu.get_barrier_semaphore()
    for h in (up, down):
        pl.semaphore_signal(barrier, inc=1, device_id={"head": h}, device_id_type=MESH)
    for b in [left, right, other] + xs_ids[1:] + ys_ids[1:] + zs_ids[1:]:
        pl.semaphore_signal(barrier, inc=1, device_id={"band": b}, device_id_type=MESH)
    rows = pl.ds(pl.multiple_of(hi * 64, 64), 64)
    loads = [pltpu.make_async_copy(src, dst, load_sem.at[i]) for i, (src, dst) in enumerate([
        (k_hbm, kvb.at[1, 0]), (v_hbm, kvb.at[1, 1]), (q_hbm, qv), (w_hbm, wv), (g_hbm, gfull.at[rows]),
        (lists_hbm, lists), (counts_hbm, counts)])]
    for c in loads[5:] + loads[:5]:
        c.start()

    column_low, column_high = x + y == 0, x + y == 6

    def ag(c, way):
        return remote(g_hbm.at[:, chunk(c)], gfull.at[rows, chunk(c)], ag_send.at[2 * c + way],
                      ag_recv.at[2 * c + way], head=(up, down)[way])

    rows_far = pl.ds(pl.multiple_of(lax.rem(hi + 2, 4) * 64, 64), 64)

    def way_of(c):
        far_low, far_high = (0, 1)
        way = lax.rem(c, 2)
        way = jnp.where(jnp.logical_and(column_low, c == 7), far_low, way)
        return jnp.where(jnp.logical_and(column_high, c == 6), far_high, way)

    def rows_from(way):
        return pl.ds(pl.multiple_of(jnp.where(way == 0, down, up) * 64, 64), 64)

    def fw(c):
        way = way_of(c)
        src = rows_from(way)
        return remote(gfull.at[src, chunk(c)], gfull.at[src, chunk(c)], fw_send.at[c], fw_recv.at[c],
                      head=jnp.where(way == 0, up, down))

    def fw_arrived(c):
        return remote(gfull.at[rows_far, chunk(c)], gfull.at[rows_far, chunk(c)], fw_send.at[c], fw_recv.at[c],
                      head=up)

    first = me * 8 - 8

    def table(b, _):
        count = counts[b]
        es = []
        for j in range(8):
            e = jnp.where(j < count, lists[b, j] - first, 24)
            eidx[b * 8 + j] = e
            es.append(e)
        for i in range(17):
            t = jnp.int32(8)
            for j in range(8):
                t = jnp.where(es[j] == b + i, j, t)
            inv_idx[b * 17 + i] = t
        return 0
    loads[5].wait()
    loads[6].wait()
    lax.fori_loop(0, 8, table, 0)
    shape = (24, 128)
    pos = (first + lax.broadcasted_iota(jnp.int32, shape, 0)) * 128 + lax.broadcasted_iota(jnp.int32, shape, 1)
    pos = jnp.clip(pos, 0, 131071).astype(F32)
    bias[...] = jnp.log(sin_to_pi(math.pi * (pos + 0.5) / 131072)) * (32 ** 0.5)

    has_left, has_right = me > 0, me < 127

    def halo(side, i):
        return remote((k_hbm, v_hbm)[i], kvb.at[side, i], kv_send.at[side + i], kv_recv.at[side + i],
                      band=right if side == 0 else left)

    pl.semaphore_wait(barrier, 14)

    @pl.when(has_right)
    def _():
        for i in range(2):
            halo(0, i).start()

    @pl.when(has_left)
    def _():
        for i in range(2):
            halo(2, i).start()

    def start_gather(ways):
        for c in range(8):
            for way in ways:
                ag(c, way).start()

    column = jnp.logical_or(column_low, column_high)
    pl.when(jnp.logical_not(column))(lambda: start_gather((0, 1)))
    pl.when(column_low)(lambda: start_gather((0,)))
    pl.when(column_high)(lambda: start_gather((1,)))

    def keys_of(side):
        def one(i, _):
            e = side * 8 + i
            prep_keys(e, kvb[side, 0, :, chunk(i)], bias[pl.ds(e, 1), :], kv_fm, k_tm)
            return 0
        lax.fori_loop(0, 8, one, 0)

    def values_of(side):
        def one(i, _):
            prep_values(side * 8 + i, kvb[side, 1, :, chunk(i)], kv_fm, v_tm)
            return 0
        lax.fori_loop(0, 8, one, 0)

    zero = jnp.zeros((64, 128), BF16)
    prep_keys(24, zero, jnp.full((1, 128), -1e30, F32), kv_fm, k_tm)
    prep_values(24, zero, kv_fm, v_tm)
    tmp[8] = jnp.zeros((128, 128), F32)
    acc[...] = jnp.zeros_like(acc)
    for i in range(4):
        loads[i].wait()
    keys_of(1)
    values_of(1)

    def arrived(side, i, prep):
        halo(side, i).wait_recv()
        prep(side)
    pl.when(core == 0)(lambda: arrived(2, 0, keys_of))
    pl.when(core == 1)(lambda: arrived(0, 0, keys_of))
    pl.when(column_low)(lambda: start_gather((1,)))
    pl.when(column_high)(lambda: start_gather((0,)))
    pl.when(jnp.logical_and(core == 0, has_left))(lambda: arrived(0, 0, keys_of))
    pl.when(jnp.logical_and(core == 1, has_right))(lambda: arrived(2, 0, keys_of))

    def ag_arrived(c, way):
        src = rows_from(way)
        return remote(gfull.at[src, chunk(c)], gfull.at[src, chunk(c)], ag_send.at[2 * c + way],
                      ag_recv.at[2 * c + way], head=jnp.where(way == 0, up, down))

    def forward_chunk(c):
        ag_arrived(c, way_of(c)).wait_recv()
        fw(c).start()

    def fwd(b, _):
        forward_block(b, qv[:, chunk(b)], eidx, kv_fm, k_tm, s_ref, p_ref, ps, inv_ref)
        for at, cs in FORWARD_AT.items():
            @pl.when(jnp.logical_and(b == at, jnp.logical_not(column)))
            def _():
                for c in cs:
                    forward_chunk(c)
        return 0
    lax.fori_loop(0, 8, fwd, 0)
    pl.when(has_left)(lambda: arrived(0, 1, values_of))
    pl.when(has_right)(lambda: arrived(2, 1, values_of))

    def attend(b, _):
        att[:, chunk(b)] = attended_block(b, eidx, kv_fm, ps)
        return 0
    lax.fori_loop(0, 8, attend, 0)

    @pl.when(column)
    def _():
        for c in range(8):
            forward_chunk(c)

    @pl.when(jnp.logical_not(column))
    def _():
        for c in FORWARD_LAST:
            forward_chunk(c)

    keep, give = core, 1 - core
    core_copy = remote(pw.at[give], rc, c_send.at[0], c_recv.at[0], band=other)
    x_copies = [remote(xs.at[x_of[d]], rx.at[d], x_send.at[d], x_recv.at[d], band=xs_ids[d]) for d in range(1, 4)]
    y_copies = [remote(mine, ry.at[d], y_send.at[d], y_recv.at[d], band=ys_ids[d]) for d in range(1, 4)]
    z_copies = [remote(ysum, rz.at[d], z_send.at[d], z_recv.at[d], band=zs_ids[d]) for d in range(1, 4)]
    my_rows = half.at[pl.ds(pl.multiple_of(x * 16, 16), 16)]
    a_copies = [remote(zsum, my_rows, a_send.at[d], a_recv.at[d], band=xs_ids[d]) for d in range(1, 4)]
    a_waits = [remote(zsum, half.at[pl.ds(pl.multiple_of(x_of[d] * 16, 16), 16)], a_send.at[d], a_recv.at[d], band=xs_ids[d]) for d in range(1, 4)]
    def columns_of(c):
        return dw_hbm.at[:, pl.ds(pl.multiple_of(c * 128, 128), 128)]

    e_copy = remote(half, columns_of(core), e_send.at[0], e_recv.at[0], band=other)
    e_wait = remote(half, columns_of(give), e_send.at[0], e_recv.at[0], band=other)
    own_copy = pltpu.make_async_copy(half, columns_of(core), out_sem.at[3])

    def sum_core():
        total = dot_nt(att[...], gfull[...])
        pw[0] = total[:, 0:128]
        pw[1] = total[:, 128:256]
        core_copy.start()

    def sum_x():
        core_copy.wait_recv()
        xs[...] = (pw[keep] + rc[...]).reshape(4, 16, 128)
        for c in x_copies:
            c.start()

    def sum_y():
        for c in x_copies:
            c.wait_recv()
        mine[...] = xs[x] + rx[1] + rx[2] + rx[3]
        for c in y_copies:
            c.start()

    def sum_z():
        for c in y_copies:
            c.wait_recv()
        ysum[...] = mine[...] + ry[1] + ry[2] + ry[3]
        for c in z_copies:
            c.start()

    def gather_x():
        for c in z_copies:
            c.wait_recv()
        t = ysum[...] + rz[1] + rz[2] + rz[3]
        zsum[...] = t
        my_rows[...] = t
        for c in a_copies:
            c.start()

    def gather_core():
        for c in a_waits:
            c.wait_recv()
        e_copy.start()
        own_copy.start()

    def rest_of_chunk(c):
        ag_arrived(c, 1 - way_of(c)).wait_recv()
        fw_arrived(c).wait_recv()

    start = jnp.where(column, START_LATE, START)

    def halo_back(side, i):
        return remote(halo_out.at[side, i], halo_in.at[side, i], ho_send.at[side * 8 + i], ho_recv.at[side * 8 + i],
                      band=(left, right)[side])

    steps = {"core": sum_core, "x": sum_x, "y": sum_y, "z": sum_z}

    def bwd(b, _):
        pl.when(b < start)(lambda: rest_of_chunk(b))

        @pl.when(b == start)
        def _():
            pl.loop(b, 8)(rest_of_chunk)

        def serve(mid):
            for at, step in SUM_AT.items():
                if at % 2 == mid:
                    pl.when(b == start + at // 2)(steps[step])
        serve(0)
        g = dot(wv[...], gfull[:, chunk(b)]).astype(BF16)
        dqv[:, chunk(b)] = backward_block(b, qv[:, chunk(b)], g, eidx, inv_idx, kv_fm, v_tm, s_ref, p_ref, ps,
                                          inv_ref, acc, tmp, lambda: serve(1))
        @pl.when(has_left)
        def _():
            halo_out[0, b] = acc[b].astype(BF16)
            halo_back(0, b).start()
        return 0
    loads[4].wait()
    lax.fori_loop(0, 8, bwd, 0)

    def send_upper(i, _):
        halo_out[1, i] = acc[16 + i].astype(BF16)
        halo_back(1, i).start()
        return 0

    @pl.when(has_right)
    def _():
        lax.fori_loop(0, 8, send_upper, 0)
    outs = [pltpu.make_async_copy(dqv, grads_hbm.at[0], out_sem.at[0])]
    outs[0].start()
    for at, step in SUM_AT.items():
        if START + at // 2 >= 8:
            pl.when(start + at // 2 >= 8)(steps[step])
    gather_x()
    gather_core()

    @pl.when(jnp.logical_not(has_right))
    def _():
        halo_in[0] = jnp.zeros((8, 128, 128), BF16)

    @pl.when(jnp.logical_not(has_left))
    def _():
        halo_in[1] = jnp.zeros((8, 128, 128), BF16)

    def finish(i, _):
        pl.when(has_right)(lambda: halo_back(0, i).wait_recv())
        pl.when(has_left)(lambda: halo_back(1, i).wait_recv())
        t = acc[8 + i] + halo_in[0, i].astype(F32) + halo_in[1, i].astype(F32)
        dkv[:, chunk(i)] = t.T.astype(BF16)
        return 0
    lax.fori_loop(0, 8, finish, 0)
    outs.append(pltpu.make_async_copy(dkv.at[0:64], grads_hbm.at[1], out_sem.at[1]))
    outs.append(pltpu.make_async_copy(dkv.at[64:128], grads_hbm.at[2], out_sem.at[2]))
    outs[1].start()
    outs[2].start()
    e_wait.wait_recv()
    own_copy.wait()
    for c in range(8):
        for way in range(2):
            ag(c, way).wait_send()
        fw(c).wait_send()

    @pl.when(has_left)
    def _():
        for c in range(8):
            halo_back(0, c).wait_send()

    pl.when(has_left)(lambda: halo(2, 0).wait_send())
    pl.when(has_left)(lambda: halo(2, 1).wait_send())

    @pl.when(has_right)
    def _():
        for c in range(8):
            halo_back(1, c).wait_send()

    pl.when(has_right)(lambda: halo(0, 0).wait_send())
    pl.when(has_right)(lambda: halo(0, 1).wait_send())

    for c in [core_copy] + x_copies + y_copies + z_copies + a_copies + [e_copy]:
        c.wait_send()
    for c in outs:
        c.wait()


FORWARD_AT = {3: (0,), 5: (1,), 7: (2, 3)}
FORWARD_LAST = (4, 5, 6, 7)
START, START_LATE = 3, 2
SUM_AT = {0: "core", 2: "x", 6: "y", 10: "z"}


def shards(queries, keys, values, grad_out, w_out, key_lists, key_counts):
    V, S, D = pltpu.VMEM, pltpu.SMEM, pltpu.SemaphoreType.DMA
    hbm = pl.BlockSpec(memory_space=pl.ANY)
    slab = jax.ShapeDtypeStruct((64, 1024), BF16)
    piece = V((16, 128), F32)
    pieces = V((4, 16, 128), F32)
    grads, dw = pl.pallas_call(
        kernel,
        out_shape=(jax.ShapeDtypeStruct((3, 64, 1024), BF16), jax.ShapeDtypeStruct((64, 256), F32)),
        in_specs=[hbm] * 7,
        out_specs=[hbm] * 2,
        scratch_shapes=[
            S((8, 8), jnp.int32), S((8,), jnp.int32), S((64,), jnp.int32), S((136,), jnp.int32), V((24, 128), F32), V((64, 1024), BF16),
            V((3, 2, 64, 1024), BF16), V((256, 1024), BF16), V((64, 256), BF16),
            V((25, 128, 128), BF16), V((25, 128, 128), BF16), V((25, 128, 128), BF16),
            V((8, 128, 256), F32), V((64, 128, 256), F32), V((64, 128, 512), BF16), V((8, 1, 256), F32),
            V((64, 1024), BF16), V((24, 128, 128), F32), V((9, 128, 128), F32), V((64, 1024), BF16), V((128, 1024), BF16),
            V((2, 8, 128, 128), BF16), V((2, 8, 128, 128), BF16),
            V((2, 64, 128), F32), V((64, 128), F32), pieces, pieces, piece, pieces, piece, pieces, piece, V((64, 128), F32),
            D((7,)), D((16,)), D((16,)), D((8,)), D((8,)), D((4,)), D((4,)), D((16,)), D((16,)),
            D((1,)), D((1,)), D((4,)), D((4,)), D((4,)), D((4,)), D((4,)), D((4,)), D((4,)), D((4,)),
            D((1,)), D((1,)), D((4,)),
        ],
        compiler_params=pltpu.CompilerParams(collective_id=0, has_side_effects=True, vmem_limit_bytes=36 * 2**20),
        name="attention_grads",
    )(*[pltpu.with_memory_space_constraint(a, pltpu.HBM) for a in (key_lists, key_counts, queries, keys, values, grad_out, w_out)])
    return grads[0], grads[1], grads[2], dw


def solution(mesh):
    split = P("head", "band")
    in_specs = (split, split, split, split, P("head", None), P("band", None), P("band"))
    out_specs = (split, split, split, P("head", None))
    return jax.shard_map(shards, mesh=mesh, in_specs=in_specs, out_specs=out_specs, check_vma=False)
```

```python
import math
import jax
import jax.numpy as jnp
from jax import lax
from jax.experimental import pallas as pl
from jax.experimental.pallas import tpu as pltpu
from jax.sharding import PartitionSpec as P

MESH = pl.DeviceIdType.MESH
F32, BF16 = jnp.float32, jnp.bfloat16
SCALE = 32 ** -0.5
EXP2_SCALE = SCALE * math.log2(math.e)
PI_HIGH = 3.1415927410125732
PI_LOW = -8.742277657347586e-08


def dot(a, b):
    return jnp.dot(a, b, preferred_element_type=F32)


def dot_nt(a, b):
    return lax.dot_general(a, b, (((1,), (1,)), ((), ())), preferred_element_type=F32)


def head_diag(m):
    return jnp.concatenate([m[0:32, 0:128], m[32:64, 128:256]], axis=0)


def block_diag(m):
    z = jnp.zeros((32, 128), m.dtype)
    return jnp.concatenate(
        [jnp.concatenate([m[0:32], z], axis=1), jnp.concatenate([z, m[32:64]], axis=1)], axis=0
    )


def sin_to_pi(x):
    y = jnp.where(x > 0.5 * math.pi, (PI_HIGH - x) + PI_LOW, x)
    z = y * y
    r = jnp.full_like(y, 1.0 / math.factorial(13))
    for n in (11, 9, 7, 5, 3):
        r = r * z + (-1.0) ** ((n - 1) // 2) / math.factorial(n)
    return y + y * (z * r)


def prep_keys(e, k, bias_row, kv_fm, k_tm):
    kv_fm[e, 0:64] = k
    high = bias_row.astype(BF16).astype(F32)
    mid = (bias_row - high).astype(BF16).astype(F32)
    low = (bias_row - high) - mid
    row = lax.broadcasted_iota(jnp.int32, (64, 128), 0)
    aug = jnp.where(row == 0, high, jnp.where(row == 1, mid, jnp.where(row == 2, low, 0.0)))
    k_tm[e] = jnp.concatenate([k, aug.astype(BF16)], axis=0).T


def prep_values(e, v, kv_fm, v_tm):
    kv_fm[e, 64:128] = v
    v_tm[e] = jnp.concatenate([v, jnp.zeros((64, 128), BF16)], axis=0).T


def forward_block(b, q, eidx, kv_fm, k_tm, s_ref, p_ref, ps, inv_ref):
    qa = jnp.concatenate([block_diag(q), jnp.ones((64, 256), BF16)], axis=0)
    es = [eidx[b * 8 + j] for j in range(8)]
    top = None
    for j in range(8):
        s = dot(k_tm[es[j]], qa)
        s_ref[j] = s
        m8 = jnp.max(s.reshape(16, 8, 256), axis=0)
        top = m8 if top is None else jnp.maximum(top, m8)
    top = jnp.max(top, axis=0, keepdims=True) * EXP2_SCALE
    total = None
    for j in range(8):
        p = jnp.exp2(s_ref[j] * EXP2_SCALE - top)
        p_ref[b * 8 + j] = p
        l8 = jnp.sum(p.reshape(16, 8, 256), axis=0)
        total = l8 if total is None else total + l8
    inv = 1.0 / jnp.sum(total, axis=0, keepdims=True)
    inv_ref[b] = inv
    for j in range(8):
        ps[b * 8 + j, :, 256:512] = (p_ref[b * 8 + j] * inv).astype(BF16)


def attended_block(b, eidx, kv_fm, ps):
    v_all = jnp.concatenate([kv_fm[eidx[b * 8 + j], 64:128] for j in range(8)], axis=1)
    p_all = ps[pl.ds(b * 8, 8), :, 256:512].reshape(1024, 256)
    return head_diag(dot(v_all, p_all)).astype(BF16)


def backward_block(b, q, g, eidx, inv_idx, kv_fm, v_tm, d_ref, p_ref, ps, inv_ref, acc, tmp, middle):
    gd = block_diag(g)
    ga = jnp.concatenate([gd, jnp.zeros((64, 256), BF16)], axis=0)
    es = [eidx[b * 8 + j] for j in range(8)]
    tot = None
    for j in range(8):
        d = dot(v_tm[es[j]], ga)
        d_ref[j] = d
        t8 = jnp.sum((p_ref[b * 8 + j] * d).reshape(16, 8, 256), axis=0)
        tot = t8 if tot is None else tot + t8
    inv = inv_ref[b]
    spread = jnp.sum(tot, axis=0, keepdims=True) * inv
    isc = inv * SCALE
    for j in range(8):
        ds = (p_ref[b * 8 + j] * isc) * (d_ref[j] - spread)
        ps[b * 8 + j, :, 0:256] = ds.astype(BF16)
    k_all = jnp.concatenate([kv_fm[es[j], 0:64] for j in range(8)], axis=1)
    d_all = ps[pl.ds(b * 8, 8), :, 0:256].reshape(1024, 256)
    dq = head_diag(dot(k_all, d_all)).astype(BF16)
    z = jnp.zeros((64, 256), BF16)
    w = jnp.concatenate(
        [jnp.concatenate([block_diag(q), z], axis=1), jnp.concatenate([z, gd], axis=1)], axis=0
    )
    middle()
    tmp[0:8] = dot(ps[pl.ds(b * 8, 8)].reshape(1024, 512), w.T).reshape(8, 128, 128)
    for i in range(17):
        acc[b + i] += tmp[inv_idx[b * 17 + i]]
    return dq


def chunk(b):
    return pl.ds(pl.multiple_of(b * 128, 128), 128)


def kernel(lists_hbm, counts_hbm, q_hbm, k_hbm, v_hbm, g_hbm, w_hbm, grads_hbm, dw_hbm,
           lists, counts, eidx, inv_idx, bias, qv, kvb, gfull, wv, kv_fm, k_tm, v_tm, s_ref, p_ref, ps, inv_ref, att, acc, tmp,
           dqv, dkv, halo_out, halo_in, pw, rc, xs, rx, mine, ry, ysum, rz, zsum, half,
           load_sem, ag_send, ag_recv, fw_send, fw_recv, kv_send, kv_recv, ho_send, ho_recv,
           c_send, c_recv, x_send, x_recv, y_send, y_recv, z_send, z_recv, a_send, a_recv, e_send, e_recv, out_sem):
    me = lax.axis_index("band")
    hi = lax.axis_index("head")
    core, x, y, z = lax.rem(me, 2), lax.rem(me // 2, 4), lax.rem(me // 8, 4), me // 32
    up, down = lax.rem(hi + 1, 4), lax.rem(hi + 3, 4)
    right, left = lax.rem(me + 1, 128), lax.rem(me + 127, 128)
    other = me + 1 - 2 * core
    x_of = [lax.rem(x + d, 4) for d in range(4)]
    xs_ids = [me + 2 * (x_of[d] - x) for d in range(4)]
    ys_ids = [me + 8 * (lax.rem(y + d, 4) - y) for d in range(4)]
    zs_ids = [me + 32 * (lax.rem(z + d, 4) - z) for d in range(4)]

    def remote(src, dst, send, recv, **to):
        return pltpu.make_async_remote_copy(src_ref=src, dst_ref=dst, send_sem=send, recv_sem=recv,
                                            device_id=to, device_id_type=MESH)

    barrier = pltpu.get_barrier_semaphore()
    for h in (up, down):
        pl.semaphore_signal(barrier, inc=1, device_id={"head": h}, device_id_type=MESH)
    for b in [left, right, other] + xs_ids[1:] + ys_ids[1:] + zs_ids[1:]:
        pl.semaphore_signal(barrier, inc=1, device_id={"band": b}, device_id_type=MESH)
    rows = pl.ds(pl.multiple_of(hi * 64, 64), 64)
    loads = [pltpu.make_async_copy(src, dst, load_sem.at[i]) for i, (src, dst) in enumerate([
        (k_hbm, kvb.at[1, 0]), (v_hbm, kvb.at[1, 1]), (q_hbm, qv), (w_hbm, wv), (g_hbm, gfull.at[rows]),
        (lists_hbm, lists), (counts_hbm, counts)])]
    for c in loads[5:] + loads[:5]:
        c.start()

    column_low, column_high = x + y == 0, x + y == 6

    def ag(c, way):
        return remote(g_hbm.at[:, chunk(c)], gfull.at[rows, chunk(c)], ag_send.at[2 * c + way],
                      ag_recv.at[2 * c + way], head=(up, down)[way])

    rows_far = pl.ds(pl.multiple_of(lax.rem(hi + 2, 4) * 64, 64), 64)

    def way_of(c):
        far_low, far_high = (0, 1)
        way = lax.rem(c, 2)
        way = jnp.where(jnp.logical_and(column_low, c == 7), far_low, way)
        return jnp.where(jnp.logical_and(column_high, c == 6), far_high, way)

    def rows_from(way):
        return pl.ds(pl.multiple_of(jnp.where(way == 0, down, up) * 64, 64), 64)

    def fw(c):
        way = way_of(c)
        src = rows_from(way)
        return remote(gfull.at[src, chunk(c)], gfull.at[src, chunk(c)], fw_send.at[c], fw_recv.at[c],
                      head=jnp.where(way == 0, up, down))

    def fw_arrived(c):
        return remote(gfull.at[rows_far, chunk(c)], gfull.at[rows_far, chunk(c)], fw_send.at[c], fw_recv.at[c],
                      head=up)

    first = me * 8 - 8

    def table(b, _):
        count = counts[b]
        es = []
        for j in range(8):
            e = jnp.where(j < count, lists[b, j] - first, 24)
            eidx[b * 8 + j] = e
            es.append(e)
        for i in range(17):
            t = jnp.int32(8)
            for j in range(8):
                t = jnp.where(es[j] == b + i, j, t)
            inv_idx[b * 17 + i] = t
        return 0
    loads[5].wait()
    loads[6].wait()
    lax.fori_loop(0, 8, table, 0)
    shape = (24, 128)
    pos = (first + lax.broadcasted_iota(jnp.int32, shape, 0)) * 128 + lax.broadcasted_iota(jnp.int32, shape, 1)
    pos = jnp.clip(pos, 0, 131071).astype(F32)
    bias[...] = jnp.log(sin_to_pi(math.pi * (pos + 0.5) / 131072)) * (32 ** 0.5)

    has_left, has_right = me > 0, me < 127

    def halo(side, i):
        return remote((k_hbm, v_hbm)[i], kvb.at[side, i], kv_send.at[side + i], kv_recv.at[side + i],
                      band=right if side == 0 else left)

    pl.semaphore_wait(barrier, 14)

    @pl.when(has_right)
    def _():
        for i in range(2):
            halo(0, i).start()

    @pl.when(has_left)
    def _():
        for i in range(2):
            halo(2, i).start()

    def start_gather(ways):
        for c in range(8):
            for way in ways:
                ag(c, way).start()

    column = jnp.logical_or(column_low, column_high)
    pl.when(jnp.logical_not(column))(lambda: start_gather((0, 1)))
    pl.when(column_low)(lambda: start_gather((0,)))
    pl.when(column_high)(lambda: start_gather((1,)))

    def keys_of(side):
        def one(i, _):
            e = side * 8 + i
            prep_keys(e, kvb[side, 0, :, chunk(i)], bias[pl.ds(e, 1), :], kv_fm, k_tm)
            return 0
        lax.fori_loop(0, 8, one, 0)

    def values_of(side):
        def one(i, _):
            prep_values(side * 8 + i, kvb[side, 1, :, chunk(i)], kv_fm, v_tm)
            return 0
        lax.fori_loop(0, 8, one, 0)

    zero = jnp.zeros((64, 128), BF16)
    prep_keys(24, zero, jnp.full((1, 128), -1e30, F32), kv_fm, k_tm)
    prep_values(24, zero, kv_fm, v_tm)
    tmp[8] = jnp.zeros((128, 128), F32)
    acc[...] = jnp.zeros_like(acc)
    for i in range(4):
        loads[i].wait()
    keys_of(1)
    values_of(1)

    def arrived(side, i, prep):
        halo(side, i).wait_recv()
        prep(side)
    pl.when(core == 0)(lambda: arrived(2, 0, keys_of))
    pl.when(core == 1)(lambda: arrived(0, 0, keys_of))
    pl.when(column_low)(lambda: start_gather((1,)))
    pl.when(column_high)(lambda: start_gather((0,)))
    pl.when(jnp.logical_and(core == 0, has_left))(lambda: arrived(0, 0, keys_of))
    pl.when(jnp.logical_and(core == 1, has_right))(lambda: arrived(2, 0, keys_of))

    def ag_arrived(c, way):
        src = rows_from(way)
        return remote(gfull.at[src, chunk(c)], gfull.at[src, chunk(c)], ag_send.at[2 * c + way],
                      ag_recv.at[2 * c + way], head=jnp.where(way == 0, up, down))

    def forward_chunk(c):
        ag_arrived(c, way_of(c)).wait_recv()
        fw(c).start()

    def fwd(b, _):
        forward_block(b, qv[:, chunk(b)], eidx, kv_fm, k_tm, s_ref, p_ref, ps, inv_ref)
        for at, cs in FORWARD_AT.items():
            @pl.when(jnp.logical_and(b == at, jnp.logical_not(column)))
            def _():
                for c in cs:
                    forward_chunk(c)
        return 0
    lax.fori_loop(0, 8, fwd, 0)
    pl.when(has_left)(lambda: arrived(0, 1, values_of))
    pl.when(has_right)(lambda: arrived(2, 1, values_of))

    def attend(b, _):
        att[:, chunk(b)] = attended_block(b, eidx, kv_fm, ps)
        return 0
    lax.fori_loop(0, 8, attend, 0)

    @pl.when(column)
    def _():
        for c in range(8):
            forward_chunk(c)

    @pl.when(jnp.logical_not(column))
    def _():
        for c in FORWARD_LAST:
            forward_chunk(c)

    keep, give = core, 1 - core
    core_copy = remote(pw.at[give], rc, c_send.at[0], c_recv.at[0], band=other)
    x_copies = [remote(xs.at[x_of[d]], rx.at[d], x_send.at[d], x_recv.at[d], band=xs_ids[d]) for d in range(1, 4)]
    y_copies = [remote(mine, ry.at[d], y_send.at[d], y_recv.at[d], band=ys_ids[d]) for d in range(1, 4)]
    z_copies = [remote(ysum, rz.at[d], z_send.at[d], z_recv.at[d], band=zs_ids[d]) for d in range(1, 4)]
    my_rows = half.at[pl.ds(pl.multiple_of(x * 16, 16), 16)]
    a_copies = [remote(zsum, my_rows, a_send.at[d], a_recv.at[d], band=xs_ids[d]) for d in range(1, 4)]
    a_waits = [remote(zsum, half.at[pl.ds(pl.multiple_of(x_of[d] * 16, 16), 16)], a_send.at[d], a_recv.at[d], band=xs_ids[d]) for d in range(1, 4)]
    def columns_of(c):
        return dw_hbm.at[:, pl.ds(pl.multiple_of(c * 128, 128), 128)]

    e_copy = remote(half, columns_of(core), e_send.at[0], e_recv.at[0], band=other)
    e_wait = remote(half, columns_of(give), e_send.at[0], e_recv.at[0], band=other)
    own_copy = pltpu.make_async_copy(half, columns_of(core), out_sem.at[3])

    def sum_core():
        total = dot_nt(att[...], gfull[...])
        pw[0] = total[:, 0:128]
        pw[1] = total[:, 128:256]
        core_copy.start()

    def sum_x():
        core_copy.wait_recv()
        xs[...] = (pw[keep] + rc[...]).reshape(4, 16, 128)
        for c in x_copies:
            c.start()

    def sum_y():
        for c in x_copies:
            c.wait_recv()
        mine[...] = xs[x] + rx[1] + rx[2] + rx[3]
        for c in y_copies:
            c.start()

    def sum_z():
        for c in y_copies:
            c.wait_recv()
        ysum[...] = mine[...] + ry[1] + ry[2] + ry[3]
        for c in z_copies:
            c.start()

    def gather_x():
        for c in z_copies:
            c.wait_recv()
        t = ysum[...] + rz[1] + rz[2] + rz[3]
        zsum[...] = t
        my_rows[...] = t
        for c in a_copies:
            c.start()

    def gather_core():
        for c in a_waits:
            c.wait_recv()
        e_copy.start()
        own_copy.start()

    def rest_of_chunk(c):
        ag_arrived(c, 1 - way_of(c)).wait_recv()
        fw_arrived(c).wait_recv()

    start = jnp.where(column, START_LATE, START)

    def halo_back(side, i):
        return remote(halo_out.at[side, i], halo_in.at[side, i], ho_send.at[side * 8 + i], ho_recv.at[side * 8 + i],
                      band=(left, right)[side])

    steps = {"core": sum_core, "x": sum_x, "y": sum_y, "z": sum_z}

    def bwd(b, _):
        pl.when(b < start)(lambda: rest_of_chunk(b))

        @pl.when(b == start)
        def _():
            pl.loop(b, 8)(rest_of_chunk)

        def serve(mid):
            for at, step in SUM_AT.items():
                if at % 2 == mid:
                    pl.when(b == start + at // 2)(steps[step])
        serve(0)
        g = dot(wv[...], gfull[:, chunk(b)]).astype(BF16)
        dqv[:, chunk(b)] = backward_block(b, qv[:, chunk(b)], g, eidx, inv_idx, kv_fm, v_tm, s_ref, p_ref, ps,
                                          inv_ref, acc, tmp, lambda: serve(1))
        @pl.when(has_left)
        def _():
            halo_out[0, b] = acc[b].astype(BF16)
            halo_back(0, b).start()
        return 0
    loads[4].wait()
    lax.fori_loop(0, 8, bwd, 0)

    def send_upper(i, _):
        halo_out[1, i] = acc[16 + i].astype(BF16)
        halo_back(1, i).start()
        return 0

    @pl.when(has_right)
    def _():
        lax.fori_loop(0, 8, send_upper, 0)
    outs = [pltpu.make_async_copy(dqv, grads_hbm.at[0], out_sem.at[0])]
    outs[0].start()
    for at, step in SUM_AT.items():
        if START + at // 2 >= 8:
            pl.when(start + at // 2 >= 8)(steps[step])
    gather_x()
    gather_core()

    @pl.when(jnp.logical_not(has_right))
    def _():
        halo_in[0] = jnp.zeros((8, 128, 128), BF16)

    @pl.when(jnp.logical_not(has_left))
    def _():
        halo_in[1] = jnp.zeros((8, 128, 128), BF16)

    def finish(i, _):
        pl.when(has_right)(lambda: halo_back(0, i).wait_recv())
        pl.when(has_left)(lambda: halo_back(1, i).wait_recv())
        t = acc[8 + i] + halo_in[0, i].astype(F32) + halo_in[1, i].astype(F32)
        dkv[:, chunk(i)] = t.T.astype(BF16)
        return 0
    lax.fori_loop(0, 8, finish, 0)
    outs.append(pltpu.make_async_copy(dkv.at[0:64], grads_hbm.at[1], out_sem.at[1]))
    outs.append(pltpu.make_async_copy(dkv.at[64:128], grads_hbm.at[2], out_sem.at[2]))
    outs[1].start()
    outs[2].start()
    e_wait.wait_recv()
    own_copy.wait()
    for c in range(8):
        for way in range(2):
            ag(c, way).wait_send()
        fw(c).wait_send()

    @pl.when(has_left)
    def _():
        for c in range(8):
            halo_back(0, c).wait_send()

    pl.when(has_left)(lambda: halo(2, 0).wait_send())
    pl.when(has_left)(lambda: halo(2, 1).wait_send())

    @pl.when(has_right)
    def _():
        for c in range(8):
            halo_back(1, c).wait_send()

    pl.when(has_right)(lambda: halo(0, 0).wait_send())
    pl.when(has_right)(lambda: halo(0, 1).wait_send())

    for c in [core_copy] + x_copies + y_copies + z_copies + a_copies + [e_copy]:
        c.wait_send()
    for c in outs:
        c.wait()


FORWARD_AT = {3: (0,), 5: (1,), 7: (2, 3)}
FORWARD_LAST = (4, 5, 6, 7)
START, START_LATE = 3, 1
SUM_AT = {0: "core", 2: "x", 6: "y", 10: "z"}


def shards(queries, keys, values, grad_out, w_out, key_lists, key_counts):
    V, S, D = pltpu.VMEM, pltpu.SMEM, pltpu.SemaphoreType.DMA
    hbm = pl.BlockSpec(memory_space=pl.ANY)
    slab = jax.ShapeDtypeStruct((64, 1024), BF16)
    piece = V((16, 128), F32)
    pieces = V((4, 16, 128), F32)
    grads, dw = pl.pallas_call(
        kernel,
        out_shape=(jax.ShapeDtypeStruct((3, 64, 1024), BF16), jax.ShapeDtypeStruct((64, 256), F32)),
        in_specs=[hbm] * 7,
        out_specs=[hbm] * 2,
        scratch_shapes=[
            S((8, 8), jnp.int32), S((8,), jnp.int32), S((64,), jnp.int32), S((136,), jnp.int32), V((24, 128), F32), V((64, 1024), BF16),
            V((3, 2, 64, 1024), BF16), V((256, 1024), BF16), V((64, 256), BF16),
            V((25, 128, 128), BF16), V((25, 128, 128), BF16), V((25, 128, 128), BF16),
            V((8, 128, 256), F32), V((64, 128, 256), F32), V((64, 128, 512), BF16), V((8, 1, 256), F32),
            V((64, 1024), BF16), V((24, 128, 128), F32), V((9, 128, 128), F32), V((64, 1024), BF16), V((128, 1024), BF16),
            V((2, 8, 128, 128), BF16), V((2, 8, 128, 128), BF16),
            V((2, 64, 128), F32), V((64, 128), F32), pieces, pieces, piece, pieces, piece, pieces, piece, V((64, 128), F32),
            D((7,)), D((16,)), D((16,)), D((8,)), D((8,)), D((4,)), D((4,)), D((16,)), D((16,)),
            D((1,)), D((1,)), D((4,)), D((4,)), D((4,)), D((4,)), D((4,)), D((4,)), D((4,)), D((4,)),
            D((1,)), D((1,)), D((4,)),
        ],
        compiler_params=pltpu.CompilerParams(collective_id=0, has_side_effects=True, vmem_limit_bytes=36 * 2**20),
        name="attention_grads",
    )(*[pltpu.with_memory_space_constraint(a, pltpu.HBM) for a in (key_lists, key_counts, queries, keys, values, grad_out, w_out)])
    return grads[0], grads[1], grads[2], dw


def solution(mesh):
    split = P("head", "band")
    in_specs = (split, split, split, split, P("head", None), P("band", None), P("band"))
    out_specs = (split, split, split, P("head", None))
    return jax.shard_map(shards, mesh=mesh, in_specs=in_specs, out_specs=out_specs, check_vma=False)
```
